32 devices in a mesh: py: 4 (over y, x), px: 8 (over z, core).
Axes of the slice: x: 2, y: 2, z: 4, core: 2. Of those that a mesh axis runs over, the one named last changes fastest.
Arguments:
- movie: bfloat16 [256, 128, 2048], P('py', 'px'), may hold values from -6 to 6
- traces: bfloat16 [4096, 2048], P('py', 'px'), may hold values from -0.125 to 0.125
- footprints: float32 [256, 128, 512], P('py', 'px'), may hold values from 0 to 1
- block_ids: int32 [4, 8, 4], P('py', 'px'), may hold values from 0 to 32, as said below
Outputs:
- updated: float32 [256, 128, 512], P('py', 'px')
The draws below stay inside these ranges and needn't reach their ends.
Inputs may be any that keep to these rules, and one draw needn't show every extreme that they name: `block_ids`: in each tile's list of 4 entries the live entries come first and are distinct block numbers below 32; the remaining entries equal 32 and mark empty slots. Every tile has at least one live entry, and some tile has all 4 live.
All inputs are finite; a program needn't handle non-finite values.
Results may differ from the reference program's by a relative error of at most 0.0003.
Values may be sent and summed in bfloat16 or wider, within the bound.
A program may use at most 64 MiB of HBM per device.

```python
import jax
import jax.numpy as jnp
from jax import lax

K = 4096
BLK = 128
SLOTS = 4
ITERS = 2
FRAMES = 2048
ROWS_DEV = 64
COLS_DEV = 16
NBLK = 32
NR = 256
NC = 128
TROWS = 4
TCOLS = 8
N_PY = 4
N_PX = 8


def draw_block_ids(key, part):
    base = jax.random.fold_in(key, 11)
    key_score, key_count, key_full = jax.random.split(base, 3)
    tiles = TROWS * TCOLS
    scores = jax.random.randint(key_score, (tiles, NBLK), 0, 2 ** 20) * NBLK + jnp.arange(NBLK, dtype=jnp.int32)[None, :]
    order = jnp.argsort(scores, axis=1)[:, :SLOTS].astype(jnp.int32)
    counts = jax.random.randint(key_count, (tiles,), 1, SLOTS + 1)
    fullest = jax.random.randint(key_full, (), 0, tiles)
    counts = jnp.where(jnp.arange(tiles) == fullest, SLOTS, counts)
    slot_index = jnp.arange(SLOTS, dtype=jnp.int32)[None, :]
    chosen = jnp.where(slot_index < counts[:, None], order, NBLK)
    return chosen.reshape(TROWS, TCOLS, SLOTS).astype(jnp.int32)


def shard_levels(stream_key, dims, shards, smallest, largest):
    level = 1.0
    for dim, blocks in shards:
        draws = jax.random.uniform(jax.random.fold_in(jax.random.fold_in(stream_key, 6), dim), (blocks,), jnp.float32, smallest / len(shards), largest / len(shards))
        level = level * jnp.repeat(jnp.exp(draws), dims[dim] // blocks).reshape((-1,) + (1,) * (len(dims) - 1 - dim))
    return level


def bell_draw(rng, shape, spread, reach, cuts=(), kind=jnp.bfloat16):
    drawn = jax.random.normal(rng, shape, jnp.float32) * spread
    if len(cuts) > 0:
        drawn = shard_levels(rng, shape, cuts, -0.22, 0.18) * drawn
    return jnp.clip(drawn, min=-reach, max=reach).astype(kind)


def setup_inputs(seed: int = 0) -> dict:
    arg_keys = jax.random.split(jax.random.key(seed), 5)
    return {
        "movie": bell_draw(arg_keys[0], (NR, NC, FRAMES), 1.0, 6.0, ((0, 4), (1, 8))),
        "traces": bell_draw(arg_keys[1], (K, FRAMES), FRAMES ** -0.5, 0.125, ((0, 4), (1, 8))),
        "footprints": jnp.clip(1.0 * jax.random.uniform(arg_keys[2], (NR, NC, SLOTS * BLK), jnp.float32) ** shard_levels(arg_keys[2], (NR, NC, SLOTS * BLK), ((0, 4), (1, 8)), -0.2, 0.2), 0.0, 1.0),
        "block_ids": draw_block_ids(jax.random.fold_in(arg_keys[4], 71), 0),
    }


def reference(movie, traces, footprints, block_ids):
    tiles = N_PY * N_PX
    pix = ROWS_DEV * COLS_DEV
    width = SLOTS * BLK
    nblk = K // BLK
    ytiles = movie.reshape(N_PY, ROWS_DEV, N_PX, COLS_DEV, FRAMES).transpose(0, 2, 1, 3, 4).reshape(tiles, pix, FRAMES)
    atiles = footprints.reshape(N_PY, ROWS_DEV, N_PX, COLS_DEV, width).transpose(0, 2, 1, 3, 4).reshape(tiles, pix, width)
    ids = block_ids.reshape(tiles, SLOTS)
    onehot = (ids[:, :, None] == jnp.arange(nblk, dtype=jnp.int32)[None, None, :]).astype(jnp.float32)
    live = lax.optimization_barrier(jnp.sum(onehot, axis=2))
    blocks = traces.reshape(nblk, BLK, FRAMES).astype(jnp.float32)
    gram_all = jnp.dot(traces, traces.T, preferred_element_type=jnp.float32).reshape(nblk, BLK, nblk, BLK)

    def per_tile(args):
        tile_movie, hot = args
        picked = jnp.einsum('sb,bnf->snf', hot, blocks).astype(jnp.bfloat16).reshape(width, FRAMES)
        cross = jnp.dot(tile_movie, picked.T, preferred_element_type=jnp.float32)
        gram = jnp.einsum('sb,bncq,dc->sndq', hot, gram_all, hot, precision=lax.Precision.HIGHEST).reshape(width, width)
        return (cross, gram)
    cross, gram = lax.map(per_tile, (ytiles, onehot))
    column_live = jnp.repeat(live, BLK, axis=1)
    denom = jnp.diagonal(gram, axis1=1, axis2=2) + 1e-06 + (1.0 - column_live)
    current = atiles * column_live[:, None, :]
    pixall = NR * NC
    for step in range(ITERS):
        for slot in range(SLOTS):
            low = slot * BLK
            columns = gram[:, :, low:low + BLK]
            resid = cross[:, :, low:low + BLK] - jnp.einsum('tpk,tkn->tpn', current, columns, precision=lax.Precision.HIGHEST)
            fresh = jnp.maximum(current[:, :, low:low + BLK] + resid / denom[:, None, low:low + BLK], 0.0)
            current = current.at[:, :, low:low + BLK].set(fresh)
        colsq = lax.optimization_barrier(jnp.sum(current * current, axis=1)).reshape(tiles, SLOTS, BLK)
        totals = jnp.einsum('tsb,tsn->bn', onehot, colsq, precision=lax.Precision.HIGHEST)
        factor = 1.0 / jnp.sqrt(totals / pixall + 1e-06)
        scale = jnp.einsum('tsb,bn->tsn', onehot, factor, precision=lax.Precision.HIGHEST).reshape(tiles, width)
        current = current * scale[:, None, :]
    return current.reshape(N_PY, N_PX, ROWS_DEV, COLS_DEV, width).transpose(0, 2, 1, 3, 4).reshape(NR, NC, width)
```

```python
import functools

import jax
import jax.numpy as jnp
from jax import lax
from jax.experimental import pallas as pl
from jax.experimental.pallas import tpu as pltpu
from jax.sharding import PartitionSpec as P

ITERS = 2
CHUNKS = 8
RELAYED = 2
MESH = pl.DeviceIdType.MESH
BF = jnp.bfloat16
F32 = jnp.float32


def split(x):
    hi = x.astype(BF)
    return hi, (x - hi.astype(F32)).astype(BF)


def mm(a, b):
    return lax.dot_general(a, b, (((1,), (0,)), ((), ())), preferred_element_type=F32)


def relayed(n_py, n_px, wid):
    return RELAYED if wid % 128 == 0 and n_px == 2 * n_py and n_py > 2 else 0


def kernel(
    n_py, n_px, movie, traces, foot, ids, cur_out, scale_out,
    y_buf, outb, recv, land, crs, hilo, id_row, id_all, id_smem, t_send, t_recv, live_row, gram_buf,
    local_sem, own_sem, id_ssem, id_rsem, g_ssem, g_rsem, x_ssem, x_rsem, t_ssem, t_rsem,
    z_buf, p_buf, outp, idp_all, idp_smem, z_sem, p_ssem, p_rsem, q_ssem, q_rsem, idp_ssem, idp_rsem,
    far_ids, far_smem, far_mat, far_ssem, far_rsem, *spans,
):
    py, px = lax.axis_index("py"), lax.axis_index("px")
    cur = cur_out
    total = n_py * n_px
    me = py * n_px + px
    loc, blk, wid = traces.shape
    nblk = loc * n_py
    slots = recv.shape[0]
    width = slots * blk
    direct = wid % 128 == 0
    pixels = y_buf.shape[0]
    step_rows = blk // CHUNKS
    relay = relayed(n_py, n_px, wid)
    chunks = CHUNKS - relay
    plane = 2 * n_py
    z, core = px // 2, lax.rem(px, 2)
    spot = py * 2 + core
    nz = n_px // 2
    rest = pl.ds(chunks * step_rows, relay * step_rows)

    owns = [
        pltpu.make_async_copy(
            traces.at[:, pl.ds(c * step_rows, step_rows), :], spans[c].at[pl.ds(py * loc, loc)], own_sem.at[c]
        )
        for c in range(chunks)
    ]
    for own in owns:
        own.start()
    if relay:
        own_z = pltpu.make_async_copy(traces.at[:, rest, :], z_buf.at[z], local_sem.at[5])
        own_z.start()
    get_foot = pltpu.make_async_copy(foot, cur, local_sem.at[1])
    get_movie = pltpu.make_async_copy(movie, y_buf, local_sem.at[2])

    lane = lax.broadcasted_iota(jnp.int32, (1, 128), 1)
    row = jnp.zeros((1, 128), jnp.int32)
    for s in range(slots):
        row = jnp.where(lane == s, ids[0, 0, s], row)
    id_row[...] = row
    id_all[px] = row
    if relay:
        idp_all[spot] = row

    barrier = pltpu.get_barrier_semaphore()

    def greet(device):
        pl.semaphore_signal(barrier, inc=1, device_id=device, device_id_type=MESH)

    def run(lo, hi, fn):
        def body(k, carry):
            fn(k)
            return carry

        lax.fori_loop(lo, hi, body, 0)

    def plane_dest(k):
        other = lax.rem(spot + k, plane)
        return other, {"py": other // 2, "px": z * 2 + lax.rem(other, 2)}

    run(1, n_px, lambda k: greet({"px": lax.rem(px + k, n_px)}))
    if relay:
        run(1, plane, lambda k: greet(plane_dest(k)[1]))
    else:
        run(1, n_py, lambda k: greet({"py": lax.rem(py + k, n_py)}))

    fill = jnp.zeros((slots, blk), jnp.int32)
    sub = lax.broadcasted_iota(jnp.int32, (slots, blk), 0)
    for s in range(slots):
        fill = jnp.where(sub == s, ids[0, 0, s], fill)
    for s in range(slots):
        alive = ((fill[s : s + 1, :] >= 0) & (fill[s : s + 1, :] < nblk)).astype(F32)
        live_row[:, s * blk : (s + 1) * blk] = alive
    pl.semaphore_wait(barrier, n_px - 1 + (plane - 1 if relay else n_py - 1))

    def id_copy(k):
        return pltpu.make_async_remote_copy(
            src_ref=id_row, dst_ref=id_all.at[px], send_sem=id_ssem.at[k], recv_sem=id_rsem.at[k],
            device_id={"px": lax.rem(px + k, n_px)}, device_id_type=MESH,
        )

    def gather_copy(c, k):
        rows = pl.ds(c * step_rows, step_rows)
        return pltpu.make_async_remote_copy(
            src_ref=traces.at[:, rows, :], dst_ref=spans[c].at[pl.ds(py * loc, loc)],
            send_sem=g_ssem.at[c, k], recv_sem=g_rsem.at[c, k],
            device_id={"py": lax.rem(py + k, n_py)}, device_id_type=MESH,
        )

    half = chunks // 2
    pair = max(slots // 2, 1)
    pieces = [(c, 1, 0, slots) for c in range(half)]
    pieces += [(half, chunks - half, s, pair) for s in range(0, slots, pair)]

    def x_copy(c, k):
        first, count, low, many = pieces[c]
        rows = pl.ds(first * step_rows, count * step_rows)
        group = pl.ds(low, many)
        dest = lax.rem(px + k, n_px)
        if direct:
            target = recv.at[group, rows, pl.ds(pl.multiple_of(px * wid, wid), wid)]
        else:
            target = land.at[px, group, rows, :]
        return pltpu.make_async_remote_copy(
            src_ref=outb.at[dest, group, rows, :],
            dst_ref=target,
            send_sem=x_ssem.at[c, k], recv_sem=x_rsem.at[c, k],
            device_id={"px": dest}, device_id_type=MESH,
        )

    def far_copy(k):
        dest = lax.rem(me + k, total)
        return pltpu.make_async_remote_copy(
            src_ref=id_row, dst_ref=far_ids.at[k - 1], send_sem=far_ssem.at[0], recv_sem=far_rsem.at[0],
            device_id={"py": dest // n_px, "px": lax.rem(dest, n_px)}, device_id_type=MESH,
        )

    def idp_copy(k):
        return pltpu.make_async_remote_copy(
            src_ref=id_row, dst_ref=idp_all.at[spot], send_sem=idp_ssem.at[k], recv_sem=idp_rsem.at[k],
            device_id=plane_dest(k)[1], device_id_type=MESH,
        )

    def chain(way, j):
        source = z - j if way == 0 else z + j
        return pltpu.make_async_remote_copy(
            src_ref=z_buf.at[source], dst_ref=z_buf.at[source],
            send_sem=z_sem.at[way, 0, j], recv_sem=z_sem.at[way, 1, j],
            device_id={"px": px + 2 if way == 0 else px - 2}, device_id_type=MESH,
        )

    def chain_sends(way, j):
        return (z - j >= 0) & (z + 1 < nz) if way == 0 else (z + j < nz) & (z - 1 >= 0)

    def chain_start(j):
        for way in range(2):
            pl.when(chain_sends(way, j))(lambda: chain(way, j).start())

    def chain_wait(j):
        for way in range(2):
            source = z - 1 - j if way == 0 else z + 1 + j
            here = source >= 0 if way == 0 else source < nz

            @pl.when(here)
            def _():
                pltpu.make_async_copy(z_buf.at[source], z_buf.at[source], z_sem.at[way, 1, j]).wait()

    def p_copy(k):
        other = lax.rem(py + k, n_py)
        return pltpu.make_async_remote_copy(
            src_ref=z_buf.at[other], dst_ref=p_buf.at[pl.ds(py * loc, loc)],
            send_sem=p_ssem.at[k], recv_sem=p_rsem.at[k], device_id={"py": other}, device_id_type=MESH,
        )

    def q_copy(k):
        other, place = plane_dest(k)
        return pltpu.make_async_remote_copy(
            src_ref=outp.at[other], dst_ref=recv.at[:, rest, pl.ds(pl.multiple_of(spot * wid, wid), wid)],
            send_sem=q_ssem.at[k], recv_sem=q_rsem.at[k], device_id=place, device_id_type=MESH,
        )

    run(1, n_px, lambda k: id_copy(k).start())
    if relay:
        run(1, plane, lambda k: idp_copy(k).start())
        own_z.wait()
        chain_start(0)
    for c in range(chunks):
        run(1, n_py, lambda k: gather_copy(c, k).start())
    get_movie.start()
    get_foot.start()
    run(1, n_px, lambda k: id_copy(k).wait())
    to_smem = pltpu.make_async_copy(id_all, id_smem, local_sem.at[3])
    to_smem.start()
    to_smem.wait()

    if relay:
        run(1, plane, lambda k: idp_copy(k).wait())
        to_plane = pltpu.make_async_copy(idp_all, idp_smem, local_sem.at[6])
        to_plane.start()
        to_plane.wait()

    def pick_plane(dest, s):
        number = idp_smem[dest, 0, s]
        ok = ((number >= 0) & (number < nblk)).astype(F32).astype(BF)
        return p_buf[jnp.minimum(jnp.maximum(number, 0), nblk - 1)] * ok

    def pick(dest, s, c):
        number = id_smem[dest, 0, s]
        ok = ((number >= 0) & (number < nblk)).astype(F32).astype(BF)
        index = jnp.minimum(jnp.maximum(number, 0), nblk - 1)
        return spans[c][index] * ok

    own_p = pltpu.make_async_copy(z_buf.at[lax.rem(py, z_buf.shape[0])], p_buf.at[pl.ds(py * loc, loc)], local_sem.at[5])
    moves = nz - 1 if relay else 0
    for c, (first, count, low, many) in enumerate(pieces):
        if c < moves:
            chain_wait(c)
            if c + 1 < moves:
                chain_start(c + 1)
            else:
                own_p.start()
                run(1, n_py, lambda k: p_copy(k).start())
        if low == 0:
            for g in range(first, first + count):
                owns[g].wait()
                run(1, n_py, lambda k: gather_copy(g, k).wait_recv())

        def route(k):
            dest = lax.rem(px + k, n_px)
            for g in range(first, first + count):
                for s in range(low, low + many):
                    outb[dest, s, pl.ds(g * step_rows, step_rows), :] = pick(dest, s, g)
            x_copy(c, k).start()

        run(1, n_px, route)
        if c == 1:
            run(1, total, lambda k: far_copy(k).start())
        for g in range(first, first + count):
            rows = pl.ds(g * step_rows, step_rows)
            for s in range(low, low + many):
                if direct:
                    recv[s, rows, pl.ds(pl.multiple_of(px * wid, wid), wid)] = pick(px, s, g)
                else:
                    land[px, s, rows, :] = pick(px, s, g)

    if relay:
        own_p.wait()
        run(1, n_py, lambda k: p_copy(k).wait_recv())

        def route_plane(k):
            other = lax.rem(spot + k, plane)
            for s in range(slots):
                outp[other, s] = pick_plane(other, s)
            q_copy(k).start()

        run(1, plane, route_plane)
        for s in range(slots):
            recv[s, rest, pl.ds(pl.multiple_of(spot * wid, wid), wid)] = pick_plane(spot, s)

    pltpu.make_async_copy(far_ids, far_ids, far_rsem.at[0]).wait()
    to_far = pltpu.make_async_copy(far_ids, far_smem, local_sem.at[7])
    to_far.start()
    get_foot.wait()
    get_movie.wait()
    live = live_row[...]
    part = min(pixels, 512)
    frames = recv.shape[2]

    def cross_part(low, i):
        at = pl.ds(pl.multiple_of(i * part, part), part)
        cols = pl.ds(low * blk, pair * blk)
        crs[at, cols] = lax.dot_general(
            y_buf[at, :], recv[low : low + pair].reshape(pair * blk, frames), (((1,), (1,)), ((), ())),
            preferred_element_type=F32,
        )

    def age(i):
        at = pl.ds(pl.multiple_of(i * part, part), part)
        cur[at, :] = cur[at, :] * live

    run(0, pixels // part, age)
    to_far.wait()

    def spread(k):
        mat = jnp.zeros((slots, blk), jnp.int32)
        for s in range(slots):
            mat = jnp.where(sub == s, far_smem[k, 0, s], mat)
        far_mat[k] = mat

    run(0, total - 1, spread)
    for c, (first, count, low, many) in enumerate(pieces):
        run(1, n_px, lambda k: x_copy(c, k).wait_recv())
        if c < half:
            continue
        if relay and low == 0:
            run(1, plane, lambda k: q_copy(k).wait_recv())
        if not direct:
            pack = 128 // wid
            for q in range(n_px // pack):
                both = [land[q * pack + j, low : low + many] for j in range(pack)]
                recv[low : low + many, :, q * 128 : (q + 1) * 128] = jnp.concatenate(both, axis=-1)
        run(0, pixels // part, lambda i: cross_part(low, i))
        near = slice(low * blk, (low + many) * blk)
        far = slice(0, (low + many) * blk)
        fresh_rows = lax.dot_general(
            recv[low : low + many].reshape(many * blk, frames), recv[: low + many].reshape((low + many) * blk, frames),
            (((1,), (1,)), ((), ())), preferred_element_type=F32,
        )
        gram_buf[near, far] = fresh_rows
        if low:
            gram_buf[: low * blk, near] = fresh_rows[:, : low * blk].T

    gram = gram_buf[...]
    eye = lax.broadcasted_iota(jnp.int32, (width, width), 0) == lax.broadcasted_iota(jnp.int32, (width, width), 1)
    denom = jnp.sum(jnp.where(eye, gram, 0.0), axis=0, keepdims=True) + 1e-06 + (1.0 - live)
    inv = 1.0 / denom
    hi, lo = split(jnp.where(eye, 1.0, 0.0) - gram * inv)
    for s in range(slots):
        hilo[s, :, :blk] = hi[:, s * blk : (s + 1) * blk]
        hilo[s, :, blk:] = lo[:, s * blk : (s + 1) * blk]
    def total_copy(step, k):
        dest = lax.rem(me + k, total)
        return pltpu.make_async_remote_copy(
            src_ref=t_send.at[step], dst_ref=t_recv.at[step, k - 1],
            send_sem=t_ssem.at[step], recv_sem=t_rsem.at[step],
            device_id={"py": dest // n_px, "px": lax.rem(dest, n_px)}, device_id_type=MESH,
        )

    scale = jnp.ones((1, width), F32)
    for step in range(ITERS):

        def sweep(i, sums, scale=scale):
            at = pl.ds(pl.multiple_of(i * part, part), part)
            now = cur[at, :] * scale
            pieces = [now[:, s * blk : (s + 1) * blk] for s in range(slots)]
            his, los = zip(*[split(p) for p in pieces])
            his, los = list(his), list(los)
            squares = []
            for s in range(slots):
                m = hilo[s]
                wide = mm(jnp.concatenate(his, axis=1), m)
                thin = mm(jnp.concatenate(los, axis=1), m[:, :blk])
                fresh = jnp.maximum(
                    crs[at, s * blk : (s + 1) * blk] * inv[:, s * blk : (s + 1) * blk] + (wide[:, :blk] + wide[:, blk:] + thin), 0.0
                )
                cur[at, s * blk : (s + 1) * blk] = fresh
                his[s], los[s] = split(fresh)
                squares.append(jnp.sum(fresh * fresh, axis=0, keepdims=True))
            return sums + jnp.concatenate(squares, axis=1)

        sums = lax.fori_loop(0, pixels // part, sweep, jnp.zeros((1, width), F32))
        for s in range(slots):
            t_send[step, s : s + 1, :] = sums[:, s * blk : (s + 1) * blk]
        run(1, total, lambda k: total_copy(step, k).start())
        if step == ITERS - 1:
            pass
        pltpu.make_async_copy(t_recv.at[step], t_recv.at[step], t_rsem.at[step]).wait()
        got = t_recv[step]
        scales = []
        for s in range(slots):
            acc = sums[:, s * blk : (s + 1) * blk]
            same = jnp.where(far_mat[...] == ids[0, 0, s], got, 0.0)
            acc = acc + jnp.sum(jnp.sum(same, axis=0), axis=0, keepdims=True)
            scales.append(1.0 / jnp.sqrt(acc / (pixels * total) + 1e-06))
        scale = jnp.concatenate(scales, axis=1) * live
    scale_out[...] = scale

    for c in range(chunks):
        run(1, n_py, lambda k: gather_copy(c, k).wait_send())
    if relay:
        for j in range(moves):
            for way in range(2):
                pl.when(chain_sends(way, j))(lambda: chain(way, j).wait_send())
        run(1, n_py, lambda k: p_copy(k).wait_send())
        run(1, plane, lambda k: q_copy(k).wait_send())
    for c in range(len(pieces)):
        run(1, n_px, lambda k: x_copy(c, k).wait_send())
    pltpu.make_async_copy(far_ids, far_ids, far_ssem.at[0]).wait()
    for step in range(ITERS):
        pltpu.make_async_copy(t_recv.at[step], t_recv.at[step], t_ssem.at[step]).wait()


def per_device(n_py, n_px, movie, traces, footprints, block_ids):
    rows, cols, frames = movie.shape
    pixels = rows * cols
    width = footprints.shape[-1]
    slots = block_ids.shape[-1]
    blk = width // slots
    wid = traces.shape[1]
    loc = traces.shape[0] // blk
    total = n_py * n_px
    relay = relayed(n_py, n_px, wid)
    part = relay * (blk // CHUNKS) or 16
    hold = n_py if relay else 1
    plane = 2 * hold
    hbm = pl.BlockSpec(memory_space=pltpu.VMEM)
    dma = pltpu.SemaphoreType.DMA
    current, scale = pl.pallas_call(
        functools.partial(kernel, n_py, n_px),
        out_shape=(
            jax.ShapeDtypeStruct((pixels, width), F32),
            jax.ShapeDtypeStruct((1, width), F32),
        ),
        in_specs=[pl.BlockSpec(memory_space=pltpu.HBM)] * 3 + [pl.BlockSpec(memory_space=pltpu.SMEM)],
        out_specs=(hbm, pl.BlockSpec(memory_space=pltpu.VMEM)),
        scratch_shapes=[
            pltpu.VMEM((pixels, frames), BF),
            pltpu.VMEM((n_px, slots, blk, wid), BF),
            pltpu.VMEM((slots, blk, frames), BF),
            pltpu.VMEM((8, 128) if wid % 128 == 0 else (n_px, slots, blk, wid), BF),
            pltpu.VMEM((pixels, width), F32),
            pltpu.VMEM((slots, width, 2 * blk), BF),
            pltpu.VMEM((1, 128), jnp.int32),
            pltpu.VMEM((n_px, 1, 128), jnp.int32),
            pltpu.SMEM((n_px, 1, 128), jnp.int32),
            pltpu.VMEM((ITERS, slots, blk), F32),
            pltpu.VMEM((ITERS, total - 1, slots, blk), F32),
            pltpu.VMEM((1, width), F32),
            pltpu.VMEM((width, width), F32),
            dma((8,)), dma((CHUNKS,)),
            dma((n_px,)), dma((n_px,)),
            dma((CHUNKS, n_py)), dma((CHUNKS, n_py)),
            dma((CHUNKS, n_px)), dma((CHUNKS, n_px)),
            dma((ITERS,)), dma((ITERS,)),
            pltpu.VMEM((hold, loc, part, wid), BF),
            pltpu.VMEM((loc * n_py, part, wid), BF),
            pltpu.VMEM((plane, slots, part, wid), BF),
            pltpu.VMEM((plane, 1, 128), jnp.int32),
            pltpu.SMEM((plane, 1, 128), jnp.int32),
            dma((2, 2, n_px)),
            dma((n_py,)), dma((n_py,)),
            dma((plane,)), dma((plane,)),
            dma((plane,)), dma((plane,)),
            pltpu.VMEM((total - 1, 1, 128), jnp.int32),
            pltpu.SMEM((total - 1, 1, 128), jnp.int32),
            pltpu.VMEM((total - 1, slots, blk), jnp.int32),
            dma((1,)), dma((1,)),
            *[pltpu.VMEM((loc * n_py, blk // CHUNKS, wid), BF) for _ in range(CHUNKS - relay)],
        ],
        compiler_params=pltpu.CompilerParams(
            collective_id=0, has_side_effects=True, vmem_limit_bytes=28 * 2**20
        ),
    )(
        pltpu.with_memory_space_constraint(movie.reshape(pixels, frames), pltpu.HBM),
        pltpu.with_memory_space_constraint(traces.reshape(loc, blk, wid), pltpu.HBM),
        pltpu.with_memory_space_constraint(footprints.reshape(pixels, width), pltpu.HBM),
        pltpu.with_memory_space_constraint(block_ids, pltpu.HBM),
    )
    return (current * scale).reshape(rows, cols, width)


def solution(mesh):
    return jax.shard_map(
        functools.partial(per_device, mesh.shape["py"], mesh.shape["px"]),
        mesh=mesh,
        in_specs=(P("py", "px", None), P("py", "px"), P("py", "px", None), P("py", "px", None)),
        out_specs=P("py", "px", None),
        check_vma=False,
    )
```

```python
import functools

import jax
import jax.numpy as jnp
from jax import lax
from jax.experimental import pallas as pl
from jax.experimental.pallas import tpu as pltpu
from jax.sharding import PartitionSpec as P

ITERS = 2
CHUNKS = 8
AHEAD = 2
LATE = 4
DIRECT = 0
PLAN = (("D", 0, 1), ("O", 4, 1), ("D", 1, 1), ("D", 2, 1), ("D", 3, 1), ("M", 4, 1), ("O", 5, 1), ("M", 5, 1), ("O", 6, 1), ("M", 6, 1), ("O", 7, 1), ("M", 7, 1))
MESH = pl.DeviceIdType.MESH
BF = jnp.bfloat16
F32 = jnp.float32


def split(x):
    hi = x.astype(BF)
    return hi, (x - hi.astype(F32)).astype(BF)


def mm(a, b):
    return lax.dot_general(a, b, (((1,), (0,)), ((), ())), preferred_element_type=F32)


def units_of(n_py, n_px, wid):
    if wid % 128 == 0 and n_px % 4 == 0 and n_py == 4:
        return PLAN
    return tuple(("D", c, 1) for c in range(CHUNKS))


def pieces_of(units, slots):
    pair = max(slots // 2, 1)
    early = len(units) - LATE
    pieces = [(u, 0, slots) for u in range(early)]
    return pieces + [(u, s, pair) for s in range(0, slots, pair) for u in range(early, len(units))]


def kernel(
    n_py, n_px, movie, traces, foot, ids, cur_out, scale_out,
    y_buf, outb, recv, land, crs, hilo, id_row, id_all, id_smem, t_send, t_recv, live_row, gram_buf,
    local_sem, own_sem, id_ssem, id_rsem, g_ssem, g_rsem, x_ssem, x_rsem, t_ssem, t_rsem, m_ssem, m_rsem,
    far_ids, far_smem, far_mat, far_ssem, far_rsem, *spans,
):
    py, px = lax.axis_index("py"), lax.axis_index("px")
    cur = cur_out
    total = n_py * n_px
    me = py * n_px + px
    loc, blk, wid = traces.shape
    nblk = loc * n_py
    slots = recv.shape[0]
    width = slots * blk
    direct = wid % 128 == 0
    pixels = y_buf.shape[0]
    step_rows = blk // CHUNKS
    units = units_of(n_py, n_px, wid)
    pieces = pieces_of(units, slots)
    pair = max(slots // 2, 1)
    nz = n_px // 2
    mirror = (nz - 1 - px // 2) * 2 + lax.rem(px, 2)
    side = n_px // 2
    base = (px // side) * side
    mine = pl.ds(py * loc, loc)
    across = [(py // 2) * 2 + 1 - lax.rem(py, 2), (1 - py // 2) * 2 + lax.rem(py, 2)]

    def rows_of(u):
        return pl.ds(units[u][1] * step_rows, units[u][2] * step_rows)

    owns = {
        u: pltpu.make_async_copy(traces.at[:, rows_of(u), :], spans[u].at[mine], own_sem.at[u])
        for u, unit in enumerate(units)
        if unit[0] != "M"
    }
    for own in owns.values():
        own.start()
    get_foot = pltpu.make_async_copy(foot, cur, local_sem.at[1])
    get_movie = pltpu.make_async_copy(movie, y_buf, local_sem.at[2])

    lane = lax.broadcasted_iota(jnp.int32, (1, 128), 1)
    row = jnp.zeros((1, 128), jnp.int32)
    for s in range(slots):
        row = jnp.where(lane == s, ids[0, 0, s], row)
    id_row[...] = row
    id_all[px] = row

    barrier = pltpu.get_barrier_semaphore()

    def greet(device):
        pl.semaphore_signal(barrier, inc=1, device_id=device, device_id_type=MESH)

    def run(lo, hi, fn):
        def body(k, carry):
            fn(k)
            return carry

        lax.fori_loop(lo, hi, body, 0)

    run(1, n_px, lambda k: greet({"px": lax.rem(px + k, n_px)}))
    run(1, n_py, lambda k: greet({"py": lax.rem(py + k, n_py)}))

    fill = jnp.zeros((slots, blk), jnp.int32)
    sub = lax.broadcasted_iota(jnp.int32, (slots, blk), 0)
    for s in range(slots):
        fill = jnp.where(sub == s, ids[0, 0, s], fill)
    for s in range(slots):
        alive = ((fill[s : s + 1, :] >= 0) & (fill[s : s + 1, :] < nblk)).astype(F32)
        live_row[:, s * blk : (s + 1) * blk] = alive
    pl.semaphore_wait(barrier, n_px - 1 + n_py - 1)

    def id_copy(k):
        return pltpu.make_async_remote_copy(
            src_ref=id_row, dst_ref=id_all.at[px], send_sem=id_ssem.at[k], recv_sem=id_rsem.at[k],
            device_id={"px": lax.rem(px + k, n_px)}, device_id_type=MESH,
        )

    def far_copy(k):
        dest = lax.rem(me + k, total)
        return pltpu.make_async_remote_copy(
            src_ref=id_row, dst_ref=far_ids.at[k - 1], send_sem=far_ssem.at[0], recv_sem=far_rsem.at[0],
            device_id={"py": dest // n_px, "px": lax.rem(dest, n_px)}, device_id_type=MESH,
        )

    def mirror_copy(u):
        return pltpu.make_async_remote_copy(
            src_ref=traces.at[:, rows_of(u), :], dst_ref=spans[u].at[mine],
            send_sem=m_ssem.at[u], recv_sem=m_rsem.at[u], device_id={"px": mirror}, device_id_type=MESH,
        )

    def held(u):
        return spans[u].at[mine] if units[u][0] == "M" else traces.at[:, rows_of(u), :]

    def gather_copy(u, k):
        return pltpu.make_async_remote_copy(
            src_ref=held(u), dst_ref=spans[u].at[mine], send_sem=g_ssem.at[u, k], recv_sem=g_rsem.at[u, k],
            device_id={"py": lax.rem(py + k, n_py)}, device_id_type=MESH,
        )

    def forwarded(u):
        return n_py == 4 and u >= DIRECT

    def near_copy(u, way):
        return pltpu.make_async_remote_copy(
            src_ref=held(u), dst_ref=spans[u].at[mine], send_sem=g_ssem.at[u, way], recv_sem=g_rsem.at[u, way],
            device_id={"py": across[way]}, device_id_type=MESH,
        )

    def far_half(u, way):
        part = spans[u].at[pl.ds(across[way] * loc + way * (loc // 2), loc // 2)]
        return pltpu.make_async_remote_copy(
            src_ref=part, dst_ref=part, send_sem=g_ssem.at[u, 2 + way], recv_sem=g_rsem.at[u, 2 + way],
            device_id={"py": across[1 - way]}, device_id_type=MESH,
        )

    def gather_start(u):
        if units[u][0] == "M":
            mirror_copy(u).wait_recv()
        if forwarded(u):
            for way in range(2):
                near_copy(u, way).start()
        else:
            run(1, n_py, lambda k: gather_copy(u, k).start())

    def gather_turn(u):
        if forwarded(u):
            for way in range(2):
                near_copy(u, way).wait_recv()
                far_half(u, way).start()

    def gather_end(u):
        if forwarded(u):
            for way in range(2):
                far_half(u, way).wait_recv()
        else:
            run(1, n_py, lambda k: gather_copy(u, k).wait_recv())
        if units[u][0] != "M":
            owns[u].wait()

    def gather_sent(u):
        if forwarded(u):
            for way in range(2):
                near_copy(u, way).wait_send()
                far_half(u, way).wait_send()
        else:
            run(1, n_py, lambda k: gather_copy(u, k).wait_send())

    def reach(u):
        return n_px if units[u][0] == "D" else side

    def x_dest(u, k):
        return lax.rem(px + k, n_px) if units[u][0] == "D" else base + lax.rem(px - base + k, side)

    def staged(u, dest):
        return n_px - 1 - dest if units[u][0] == "M" else dest

    def frames_at(u):
        source = mirror if units[u][0] == "M" else px
        return pl.ds(pl.multiple_of(source * wid, wid), wid)

    def x_copy(c, k):
        u, low, many = pieces[c]
        rows = rows_of(u)
        group = pl.ds(low, many)
        dest = x_dest(u, k)
        target = recv.at[group, rows, frames_at(u)] if direct else land.at[px, group, rows, :]
        return pltpu.make_async_remote_copy(
            src_ref=outb.at[staged(u, dest), group, rows, :],
            dst_ref=target,
            send_sem=x_ssem.at[c, k], recv_sem=x_rsem.at[c, k],
            device_id={"px": dest}, device_id_type=MESH,
        )

    run(1, n_px, lambda k: id_copy(k).start())
    for u in range(AHEAD):
        if u == AHEAD - 1:
            for v, unit in enumerate(units):
                if unit[0] == "M":
                    mirror_copy(v).start()
        gather_start(u)
    get_movie.start()
    get_foot.start()
    run(1, n_px, lambda k: id_copy(k).wait())
    to_smem = pltpu.make_async_copy(id_all, id_smem, local_sem.at[3])
    to_smem.start()
    to_smem.wait()

    def pick(dest, s, u):
        number = id_smem[dest, 0, s]
        ok = ((number >= 0) & (number < nblk)).astype(F32).astype(BF)
        index = jnp.minimum(jnp.maximum(number, 0), nblk - 1)
        return spans[u][index] * ok

    def deal(c):
        u, low, many = pieces[c]
        rows = rows_of(u)

        def route(k):
            dest = x_dest(u, k)
            for s in range(low, low + many):
                outb[staged(u, dest), s, rows, :] = pick(dest, s, u)
            x_copy(c, k).start()

        run(1, reach(u), route)
        for s in range(low, low + many):
            if direct:
                recv[s, rows, frames_at(u)] = pick(px, s, u)
            else:
                land[px, s, rows, :] = pick(px, s, u)

    for u in range(len(units) + 1):
        if u < len(units):
            gather_turn(u)
            if u + AHEAD < len(units):
                gather_start(u + AHEAD)
        if u:
            gather_end(u - 1)
            deal(u - 1)
        if u == 2:
            run(1, total, lambda k: far_copy(k).start())
    for c in range(len(units), len(pieces)):
        deal(c)

    pltpu.make_async_copy(far_ids, far_ids, far_rsem.at[0]).wait()
    to_far = pltpu.make_async_copy(far_ids, far_smem, local_sem.at[7])
    to_far.start()
    get_foot.wait()
    get_movie.wait()
    live = live_row[...]
    part = min(pixels, 512)
    frames = recv.shape[2]

    def cross_part(low, i):
        at = pl.ds(pl.multiple_of(i * part, part), part)
        cols = pl.ds(low * blk, pair * blk)
        crs[at, cols] = lax.dot_general(
            y_buf[at, :], recv[low : low + pair].reshape(pair * blk, frames), (((1,), (1,)), ((), ())),
            preferred_element_type=F32,
        )

    def age(i):
        at = pl.ds(pl.multiple_of(i * part, part), part)
        cur[at, :] = cur[at, :] * live

    run(0, pixels // part, age)
    to_far.wait()

    def spread(k):
        mat = jnp.zeros((slots, blk), jnp.int32)
        for s in range(slots):
            mat = jnp.where(sub == s, far_smem[k, 0, s], mat)
        far_mat[k] = mat

    run(0, total - 1, spread)
    for c, (u, low, many) in enumerate(pieces):
        run(1, reach(u), lambda k: x_copy(c, k).wait_recv())
        if many == slots > 1 or u < len(units) - 1:
            continue
        if not direct:
            pack = 128 // wid
            for q in range(n_px // pack):
                both = [land[q * pack + j, low : low + many] for j in range(pack)]
                recv[low : low + many, :, q * 128 : (q + 1) * 128] = jnp.concatenate(both, axis=-1)
        run(0, pixels // part, lambda i: cross_part(low, i))
        near = slice(low * blk, (low + many) * blk)
        far = slice(0, (low + many) * blk)
        fresh_rows = lax.dot_general(
            recv[low : low + many].reshape(many * blk, frames), recv[: low + many].reshape((low + many) * blk, frames),
            (((1,), (1,)), ((), ())), preferred_element_type=F32,
        )
        gram_buf[near, far] = fresh_rows
        if low:
            gram_buf[: low * blk, near] = fresh_rows[:, : low * blk].T

    gram = gram_buf[...]
    eye = lax.broadcasted_iota(jnp.int32, (width, width), 0) == lax.broadcasted_iota(jnp.int32, (width, width), 1)
    denom = jnp.sum(jnp.where(eye, gram, 0.0), axis=0, keepdims=True) + 1e-06 + (1.0 - live)
    inv = 1.0 / denom
    hi, lo = split(jnp.where(eye, 1.0, 0.0) - gram * inv)
    for s in range(slots):
        hilo[s, :, :blk] = hi[:, s * blk : (s + 1) * blk]
        hilo[s, :, blk:] = lo[:, s * blk : (s + 1) * blk]
    def total_copy(step, k):
        dest = lax.rem(me + k, total)
        return pltpu.make_async_remote_copy(
            src_ref=t_send.at[step], dst_ref=t_recv.at[step, k - 1],
            send_sem=t_ssem.at[step], recv_sem=t_rsem.at[step],
            device_id={"py": dest // n_px, "px": lax.rem(dest, n_px)}, device_id_type=MESH,
        )

    scale = jnp.ones((1, width), F32)
    for step in range(ITERS):

        def sweep(i, sums, scale=scale):
            at = pl.ds(pl.multiple_of(i * part, part), part)
            now = cur[at, :] * scale
            pieces = [now[:, s * blk : (s + 1) * blk] for s in range(slots)]
            his, los = zip(*[split(p) for p in pieces])
            his, los = list(his), list(los)
            squares = []
            for s in range(slots):
                m = hilo[s]
                wide = mm(jnp.concatenate(his, axis=1), m)
                thin = mm(jnp.concatenate(los, axis=1), m[:, :blk])
                fresh = jnp.maximum(
                    crs[at, s * blk : (s + 1) * blk] * inv[:, s * blk : (s + 1) * blk] + (wide[:, :blk] + wide[:, blk:] + thin), 0.0
                )
                cur[at, s * blk : (s + 1) * blk] = fresh
                his[s], los[s] = split(fresh)
                squares.append(jnp.sum(fresh * fresh, axis=0, keepdims=True))
            return sums + jnp.concatenate(squares, axis=1)

        sums = lax.fori_loop(0, pixels // part, sweep, jnp.zeros((1, width), F32))
        for s in range(slots):
            t_send[step, s : s + 1, :] = sums[:, s * blk : (s + 1) * blk]
        run(1, total, lambda k: total_copy(step, k).start())
        if step == ITERS - 1:
            pass
        pltpu.make_async_copy(t_recv.at[step], t_recv.at[step], t_rsem.at[step]).wait()
        got = t_recv[step]
        scales = []
        for s in range(slots):
            acc = sums[:, s * blk : (s + 1) * blk]
            same = jnp.where(far_mat[...] == ids[0, 0, s], got, 0.0)
            acc = acc + jnp.sum(jnp.sum(same, axis=0), axis=0, keepdims=True)
            scales.append(1.0 / jnp.sqrt(acc / (pixels * total) + 1e-06))
        scale = jnp.concatenate(scales, axis=1) * live
    scale_out[...] = scale

    for u, unit in enumerate(units):
        gather_sent(u)
        if unit[0] == "M":
            mirror_copy(u).wait_send()
    for c, (u, low, many) in enumerate(pieces):
        run(1, reach(u), lambda k: x_copy(c, k).wait_send())
    pltpu.make_async_copy(far_ids, far_ids, far_ssem.at[0]).wait()
    for step in range(ITERS):
        pltpu.make_async_copy(t_recv.at[step], t_recv.at[step], t_ssem.at[step]).wait()


def per_device(n_py, n_px, movie, traces, footprints, block_ids):
    rows, cols, frames = movie.shape
    pixels = rows * cols
    width = footprints.shape[-1]
    slots = block_ids.shape[-1]
    blk = width // slots
    wid = traces.shape[1]
    loc = traces.shape[0] // blk
    total = n_py * n_px
    units = units_of(n_py, n_px, wid)
    pieces = pieces_of(units, slots)
    hbm = pl.BlockSpec(memory_space=pltpu.VMEM)
    dma = pltpu.SemaphoreType.DMA
    current, scale = pl.pallas_call(
        functools.partial(kernel, n_py, n_px),
        out_shape=(
            jax.ShapeDtypeStruct((pixels, width), F32),
            jax.ShapeDtypeStruct((1, width), F32),
        ),
        in_specs=[pl.BlockSpec(memory_space=pltpu.HBM)] * 3 + [pl.BlockSpec(memory_space=pltpu.SMEM)],
        out_specs=(hbm, pl.BlockSpec(memory_space=pltpu.VMEM)),
        scratch_shapes=[
            pltpu.VMEM((pixels, frames), BF),
            pltpu.VMEM((n_px, slots, blk, wid), BF),
            pltpu.VMEM((slots, blk, frames), BF),
            pltpu.VMEM((8, 128) if wid % 128 == 0 else (n_px, slots, blk, wid), BF),
            pltpu.VMEM((pixels, width), F32),
            pltpu.VMEM((slots, width, 2 * blk), BF),
            pltpu.VMEM((1, 128), jnp.int32),
            pltpu.VMEM((n_px, 1, 128), jnp.int32),
            pltpu.SMEM((n_px, 1, 128), jnp.int32),
            pltpu.VMEM((ITERS, slots, blk), F32),
            pltpu.VMEM((ITERS, total - 1, slots, blk), F32),
            pltpu.VMEM((1, width), F32),
            pltpu.VMEM((width, width), F32),
            dma((8,)), dma((len(units),)),
            dma((n_px,)), dma((n_px,)),
            dma((len(units), n_py)), dma((len(units), n_py)),
            dma((len(pieces), n_px)), dma((len(pieces), n_px)),
            dma((ITERS,)), dma((ITERS,)),
            dma((len(units),)), dma((len(units),)),
            pltpu.VMEM((total - 1, 1, 128), jnp.int32),
            pltpu.SMEM((total - 1, 1, 128), jnp.int32),
            pltpu.VMEM((total - 1, slots, blk), jnp.int32),
            dma((1,)), dma((1,)),
            *[pltpu.VMEM((loc * n_py, unit[2] * (blk // CHUNKS), wid), BF) for unit in units],
        ],
        compiler_params=pltpu.CompilerParams(
            collective_id=0, has_side_effects=True, vmem_limit_bytes=28 * 2**20
        ),
    )(
        pltpu.with_memory_space_constraint(movie.reshape(pixels, frames), pltpu.HBM),
        pltpu.with_memory_space_constraint(traces.reshape(loc, blk, wid), pltpu.HBM),
        pltpu.with_memory_space_constraint(footprints.reshape(pixels, width), pltpu.HBM),
        pltpu.with_memory_space_constraint(block_ids, pltpu.HBM),
    )
    return (current * scale).reshape(rows, cols, width)


def solution(mesh):
    return jax.shard_map(
        functools.partial(per_device, mesh.shape["py"], mesh.shape["px"]),
        mesh=mesh,
        in_specs=(P("py", "px", None), P("py", "px"), P("py", "px", None), P("py", "px", None)),
        out_specs=P("py", "px", None),
        check_vma=False,
    )
```

```python
import functools

import jax
import jax.numpy as jnp
from jax import lax
from jax.experimental import pallas as pl
from jax.experimental.pallas import tpu as pltpu
from jax.sharding import PartitionSpec as P

ITERS = 2
CHUNKS = 8
AHEAD = 2
LATE = 4
DIRECT = 0
PLAN = (("D", 0, 1), ("O", 4, 1), ("D", 1, 1), ("D", 2, 1), ("D", 3, 1), ("M", 4, 1), ("O", 5, 1), ("M", 5, 1), ("O", 6, 1), ("M", 6, 1), ("O", 7, 1), ("M", 7, 1))
MESH = pl.DeviceIdType.MESH
BF = jnp.bfloat16
F32 = jnp.float32


def split(x):
    hi = x.astype(BF)
    return hi, (x - hi.astype(F32)).astype(BF)


def mm(a, b):
    return lax.dot_general(a, b, (((1,), (0,)), ((), ())), preferred_element_type=F32)


def units_of(n_py, n_px, wid):
    if wid % 128 == 0 and n_px % 4 == 0 and n_py == 4:
        return PLAN
    return tuple(("D", c, 1) for c in range(CHUNKS))


def pieces_of(units, slots):
    pair = max(slots // 2, 1)
    early = len(units) - LATE
    pieces = [(u, 0, slots) for u in range(early)]
    return pieces + [(u, s, pair) for s in range(0, slots, pair) for u in range(early, len(units))]


def kernel(
    n_py, n_px, movie, traces, foot, ids, cur_out, scale_out,
    y_buf, outb, recv, land, crs, hilo, id_row, id_all, id_smem, t_send, t_recv, live_row, gram_buf,
    local_sem, own_sem, id_ssem, id_rsem, g_ssem, g_rsem, x_ssem, x_rsem, t_ssem, t_rsem, m_ssem, m_rsem,
    far_ids, far_smem, far_mat, far_ssem, far_rsem, *spans,
):
    py, px = lax.axis_index("py"), lax.axis_index("px")
    cur = cur_out
    total = n_py * n_px
    me = py * n_px + px
    loc, blk, wid = traces.shape
    nblk = loc * n_py
    slots = recv.shape[0]
    width = slots * blk
    direct = wid % 128 == 0
    pixels = y_buf.shape[0]
    step_rows = blk // CHUNKS
    units = units_of(n_py, n_px, wid)
    pieces = pieces_of(units, slots)
    pair = max(slots // 2, 1)
    nz = n_px // 2
    mirror = (nz - 1 - px // 2) * 2 + lax.rem(px, 2)
    side = n_px // 2
    base = (px // side) * side
    mine = pl.ds(py * loc, loc)
    across = [(py // 2) * 2 + 1 - lax.rem(py, 2), (1 - py // 2) * 2 + lax.rem(py, 2)]

    def rows_of(u):
        return pl.ds(units[u][1] * step_rows, units[u][2] * step_rows)

    barrier = pltpu.get_barrier_semaphore()

    def greet(device):
        pl.semaphore_signal(barrier, inc=1, device_id=device, device_id_type=MESH)

    def run(lo, hi, fn):
        def body(k, carry):
            fn(k)
            return carry

        lax.fori_loop(lo, hi, body, 0)

    run(1, n_px, lambda k: greet({"px": lax.rem(px + k, n_px)}))
    run(1, n_py, lambda k: greet({"py": lax.rem(py + k, n_py)}))

    owns = {
        u: pltpu.make_async_copy(traces.at[:, rows_of(u), :], spans[u].at[mine], own_sem.at[u])
        for u, unit in enumerate(units)
        if unit[0] != "M"
    }
    for own in owns.values():
        own.start()
    get_foot = pltpu.make_async_copy(foot, cur, local_sem.at[1])
    get_movie = pltpu.make_async_copy(movie, y_buf, local_sem.at[2])

    lane = lax.broadcasted_iota(jnp.int32, (1, 128), 1)
    row = jnp.zeros((1, 128), jnp.int32)
    for s in range(slots):
        row = jnp.where(lane == s, ids[0, 0, s], row)
    id_row[...] = row
    id_all[px] = row

    fill = jnp.zeros((slots, blk), jnp.int32)
    sub = lax.broadcasted_iota(jnp.int32, (slots, blk), 0)
    for s in range(slots):
        fill = jnp.where(sub == s, ids[0, 0, s], fill)
    for s in range(slots):
        alive = ((fill[s : s + 1, :] >= 0) & (fill[s : s + 1, :] < nblk)).astype(F32)
        live_row[:, s * blk : (s + 1) * blk] = alive
    pl.semaphore_wait(barrier, n_px - 1 + n_py - 1)

    def id_copy(k):
        return pltpu.make_async_remote_copy(
            src_ref=id_row, dst_ref=id_all.at[px], send_sem=id_ssem.at[k], recv_sem=id_rsem.at[k],
            device_id={"px": lax.rem(px + k, n_px)}, device_id_type=MESH,
        )

    def far_copy(k):
        dest = lax.rem(me + k, total)
        return pltpu.make_async_remote_copy(
            src_ref=id_row, dst_ref=far_ids.at[k - 1], send_sem=far_ssem.at[0], recv_sem=far_rsem.at[0],
            device_id={"py": dest // n_px, "px": lax.rem(dest, n_px)}, device_id_type=MESH,
        )

    def mirror_copy(u):
        return pltpu.make_async_remote_copy(
            src_ref=traces.at[:, rows_of(u), :], dst_ref=spans[u].at[mine],
            send_sem=m_ssem.at[u], recv_sem=m_rsem.at[u], device_id={"px": mirror}, device_id_type=MESH,
        )

    def held(u):
        return spans[u].at[mine] if units[u][0] == "M" else traces.at[:, rows_of(u), :]

    def gather_copy(u, k):
        return pltpu.make_async_remote_copy(
            src_ref=held(u), dst_ref=spans[u].at[mine], send_sem=g_ssem.at[u, k], recv_sem=g_rsem.at[u, k],
            device_id={"py": lax.rem(py + k, n_py)}, device_id_type=MESH,
        )

    def forwarded(u):
        return n_py == 4 and u >= DIRECT

    def near_copy(u, way):
        return pltpu.make_async_remote_copy(
            src_ref=held(u), dst_ref=spans[u].at[mine], send_sem=g_ssem.at[u, way], recv_sem=g_rsem.at[u, way],
            device_id={"py": across[way]}, device_id_type=MESH,
        )

    def far_half(u, way):
        part = spans[u].at[pl.ds(across[way] * loc + way * (loc // 2), loc // 2)]
        return pltpu.make_async_remote_copy(
            src_ref=part, dst_ref=part, send_sem=g_ssem.at[u, 2 + way], recv_sem=g_rsem.at[u, 2 + way],
            device_id={"py": across[1 - way]}, device_id_type=MESH,
        )

    def gather_start(u):
        if units[u][0] == "M":
            mirror_copy(u).wait_recv()
        if forwarded(u):
            for way in range(2):
                near_copy(u, way).start()
        else:
            run(1, n_py, lambda k: gather_copy(u, k).start())

    def gather_turn(u):
        if forwarded(u):
            for way in range(2):
                near_copy(u, way).wait_recv()
                far_half(u, way).start()

    def gather_end(u):
        if forwarded(u):
            for way in range(2):
                far_half(u, way).wait_recv()
        else:
            run(1, n_py, lambda k: gather_copy(u, k).wait_recv())
        if units[u][0] != "M":
            owns[u].wait()

    def gather_sent(u):
        if forwarded(u):
            for way in range(2):
                near_copy(u, way).wait_send()
                far_half(u, way).wait_send()
        else:
            run(1, n_py, lambda k: gather_copy(u, k).wait_send())

    def reach(u):
        return n_px if units[u][0] == "D" else side

    def x_dest(u, k):
        return lax.rem(px + k, n_px) if units[u][0] == "D" else base + lax.rem(px - base + k, side)

    def staged(u, dest):
        return n_px - 1 - dest if units[u][0] == "M" else dest

    def frames_at(u):
        source = mirror if units[u][0] == "M" else px
        return pl.ds(pl.multiple_of(source * wid, wid), wid)

    def x_copy(c, k):
        u, low, many = pieces[c]
        rows = rows_of(u)
        group = pl.ds(low, many)
        dest = x_dest(u, k)
        target = recv.at[group, rows, frames_at(u)] if direct else land.at[px, group, rows, :]
        return pltpu.make_async_remote_copy(
            src_ref=outb.at[staged(u, dest), group, rows, :],
            dst_ref=target,
            send_sem=x_ssem.at[c, k], recv_sem=x_rsem.at[c, k],
            device_id={"px": dest}, device_id_type=MESH,
        )

    run(1, n_px, lambda k: id_copy(k).start())
    for u in range(AHEAD):
        if u == AHEAD - 1:
            for v, unit in enumerate(units):
                if unit[0] == "M":
                    mirror_copy(v).start()
        gather_start(u)
    get_movie.start()
    get_foot.start()
    run(1, n_px, lambda k: id_copy(k).wait())
    to_smem = pltpu.make_async_copy(id_all, id_smem, local_sem.at[3])
    to_smem.start()
    to_smem.wait()

    def pick(dest, s, u):
        number = id_smem[dest, 0, s]
        ok = ((number >= 0) & (number < nblk)).astype(F32).astype(BF)
        index = jnp.minimum(jnp.maximum(number, 0), nblk - 1)
        return spans[u][index] * ok

    def deal(c):
        u, low, many = pieces[c]
        rows = rows_of(u)

        def route(k):
            dest = x_dest(u, k)
            for s in range(low, low + many):
                outb[staged(u, dest), s, rows, :] = pick(dest, s, u)
            x_copy(c, k).start()

        run(1, reach(u), route)
        for s in range(low, low + many):
            if direct:
                recv[s, rows, frames_at(u)] = pick(px, s, u)
            else:
                land[px, s, rows, :] = pick(px, s, u)

    for u in range(len(units) + 1):
        if u < len(units):
            gather_turn(u)
            if u + AHEAD < len(units):
                gather_start(u + AHEAD)
        if u:
            gather_end(u - 1)
            deal(u - 1)
        if u == 2:
            run(1, total, lambda k: far_copy(k).start())
    for c in range(len(units), len(pieces)):
        deal(c)

    pltpu.make_async_copy(far_ids, far_ids, far_rsem.at[0]).wait()
    to_far = pltpu.make_async_copy(far_ids, far_smem, local_sem.at[7])
    to_far.start()
    get_foot.wait()
    get_movie.wait()
    live = live_row[...]
    part = min(pixels, 512)
    frames = recv.shape[2]

    def cross_part(low, i):
        at = pl.ds(pl.multiple_of(i * part, part), part)
        cols = pl.ds(low * blk, pair * blk)
        crs[at, cols] = lax.dot_general(
            y_buf[at, :], recv[low : low + pair].reshape(pair * blk, frames), (((1,), (1,)), ((), ())),
            preferred_element_type=F32,
        )

    def age(i):
        at = pl.ds(pl.multiple_of(i * part, part), part)
        cur[at, :] = cur[at, :] * live

    run(0, pixels // part, age)
    to_far.wait()

    def spread(k):
        mat = jnp.zeros((slots, blk), jnp.int32)
        for s in range(slots):
            mat = jnp.where(sub == s, far_smem[k, 0, s], mat)
        far_mat[k] = mat

    run(0, total - 1, spread)
    for c, (u, low, many) in enumerate(pieces):
        run(1, reach(u), lambda k: x_copy(c, k).wait_recv())
        if many == slots > 1 or u < len(units) - 1:
            continue
        if not direct:
            pack = 128 // wid
            for q in range(n_px // pack):
                both = [land[q * pack + j, low : low + many] for j in range(pack)]
                recv[low : low + many, :, q * 128 : (q + 1) * 128] = jnp.concatenate(both, axis=-1)
        run(0, pixels // part, lambda i: cross_part(low, i))
        near = slice(low * blk, (low + many) * blk)
        far = slice(0, (low + many) * blk)
        fresh_rows = lax.dot_general(
            recv[low : low + many].reshape(many * blk, frames), recv[: low + many].reshape((low + many) * blk, frames),
            (((1,), (1,)), ((), ())), preferred_element_type=F32,
        )
        gram_buf[near, far] = fresh_rows
        if low:
            gram_buf[: low * blk, near] = fresh_rows[:, : low * blk].T

    gram = gram_buf[...]
    eye = lax.broadcasted_iota(jnp.int32, (width, width), 0) == lax.broadcasted_iota(jnp.int32, (width, width), 1)
    denom = jnp.sum(jnp.where(eye, gram, 0.0), axis=0, keepdims=True) + 1e-06 + (1.0 - live)
    inv = 1.0 / denom
    hi, lo = split(jnp.where(eye, 1.0, 0.0) - gram * inv)
    for s in range(slots):
        hilo[s, :, :blk] = hi[:, s * blk : (s + 1) * blk]
        hilo[s, :, blk:] = lo[:, s * blk : (s + 1) * blk]
    def total_copy(step, k):
        dest = lax.rem(me + k, total)
        return pltpu.make_async_remote_copy(
            src_ref=t_send.at[step], dst_ref=t_recv.at[step, k - 1],
            send_sem=t_ssem.at[step], recv_sem=t_rsem.at[step],
            device_id={"py": dest // n_px, "px": lax.rem(dest, n_px)}, device_id_type=MESH,
        )

    scale = jnp.ones((1, width), F32)
    for step in range(ITERS):

        def sweep(i, sums, scale=scale):
            at = pl.ds(pl.multiple_of(i * part, part), part)
            now = cur[at, :] * scale
            pieces = [now[:, s * blk : (s + 1) * blk] for s in range(slots)]
            his, los = zip(*[split(p) for p in pieces])
            his, los = list(his), list(los)
            squares = []
            for s in range(slots):
                m = hilo[s]
                wide = mm(jnp.concatenate(his, axis=1), m)
                thin = mm(jnp.concatenate(los, axis=1), m[:, :blk])
                fresh = jnp.maximum(
                    crs[at, s * blk : (s + 1) * blk] * inv[:, s * blk : (s + 1) * blk] + (wide[:, :blk] + wide[:, blk:] + thin), 0.0
                )
                cur[at, s * blk : (s + 1) * blk] = fresh
                his[s], los[s] = split(fresh)
                squares.append(jnp.sum(fresh * fresh, axis=0, keepdims=True))
            return sums + jnp.concatenate(squares, axis=1)

        sums = lax.fori_loop(0, pixels // part, sweep, jnp.zeros((1, width), F32))
        for s in range(slots):
            t_send[step, s : s + 1, :] = sums[:, s * blk : (s + 1) * blk]
        run(1, total, lambda k: total_copy(step, k).start())
        if step == 0:
            for u, unit in enumerate(units):
                gather_sent(u)
                if unit[0] == "M":
                    mirror_copy(u).wait_send()
            for c, (u, low, many) in enumerate(pieces):
                run(1, reach(u), lambda k: x_copy(c, k).wait_send())
            pltpu.make_async_copy(far_ids, far_ids, far_ssem.at[0]).wait()
        pltpu.make_async_copy(t_recv.at[step], t_recv.at[step], t_rsem.at[step]).wait()
        got = t_recv[step]
        scales = []
        for s in range(slots):
            acc = sums[:, s * blk : (s + 1) * blk]
            same = jnp.where(far_mat[...] == ids[0, 0, s], got, 0.0)
            acc = acc + jnp.sum(jnp.sum(same, axis=0), axis=0, keepdims=True)
            scales.append(1.0 / jnp.sqrt(acc / (pixels * total) + 1e-06))
        scale = jnp.concatenate(scales, axis=1) * live
    scale_out[...] = scale

    for step in range(ITERS):
        pltpu.make_async_copy(t_recv.at[step], t_recv.at[step], t_ssem.at[step]).wait()


def per_device(n_py, n_px, movie, traces, footprints, block_ids):
    rows, cols, frames = movie.shape
    pixels = rows * cols
    width = footprints.shape[-1]
    slots = block_ids.shape[-1]
    blk = width // slots
    wid = traces.shape[1]
    loc = traces.shape[0] // blk
    total = n_py * n_px
    units = units_of(n_py, n_px, wid)
    pieces = pieces_of(units, slots)
    hbm = pl.BlockSpec(memory_space=pltpu.VMEM)
    dma = pltpu.SemaphoreType.DMA
    current, scale = pl.pallas_call(
        functools.partial(kernel, n_py, n_px),
        out_shape=(
            jax.ShapeDtypeStruct((pixels, width), F32),
            jax.ShapeDtypeStruct((1, width), F32),
        ),
        in_specs=[pl.BlockSpec(memory_space=pltpu.HBM)] * 3 + [pl.BlockSpec(memory_space=pltpu.SMEM)],
        out_specs=(hbm, pl.BlockSpec(memory_space=pltpu.VMEM)),
        scratch_shapes=[
            pltpu.VMEM((pixels, frames), BF),
            pltpu.VMEM((n_px, slots, blk, wid), BF),
            pltpu.VMEM((slots, blk, frames), BF),
            pltpu.VMEM((8, 128) if wid % 128 == 0 else (n_px, slots, blk, wid), BF),
            pltpu.VMEM((pixels, width), F32),
            pltpu.VMEM((slots, width, 2 * blk), BF),
            pltpu.VMEM((1, 128), jnp.int32),
            pltpu.VMEM((n_px, 1, 128), jnp.int32),
            pltpu.SMEM((n_px, 1, 128), jnp.int32),
            pltpu.VMEM((ITERS, slots, blk), F32),
            pltpu.VMEM((ITERS, total - 1, slots, blk), F32),
            pltpu.VMEM((1, width), F32),
            pltpu.VMEM((width, width), F32),
            dma((8,)), dma((len(units),)),
            dma((n_px,)), dma((n_px,)),
            dma((len(units), n_py)), dma((len(units), n_py)),
            dma((len(pieces), n_px)), dma((len(pieces), n_px)),
            dma((ITERS,)), dma((ITERS,)),
            dma((len(units),)), dma((len(units),)),
            pltpu.VMEM((total - 1, 1, 128), jnp.int32),
            pltpu.SMEM((total - 1, 1, 128), jnp.int32),
            pltpu.VMEM((total - 1, slots, blk), jnp.int32),
            dma((1,)), dma((1,)),
            *[pltpu.VMEM((loc * n_py, unit[2] * (blk // CHUNKS), wid), BF) for unit in units],
        ],
        compiler_params=pltpu.CompilerParams(
            collective_id=0, has_side_effects=True, vmem_limit_bytes=28 * 2**20
        ),
    )(
        pltpu.with_memory_space_constraint(movie.reshape(pixels, frames), pltpu.HBM),
        pltpu.with_memory_space_constraint(traces.reshape(loc, blk, wid), pltpu.HBM),
        pltpu.with_memory_space_constraint(footprints.reshape(pixels, width), pltpu.HBM),
        pltpu.with_memory_space_constraint(block_ids, pltpu.HBM),
    )
    return (current * scale).reshape(rows, cols, width)


def solution(mesh):
    return jax.shard_map(
        functools.partial(per_device, mesh.shape["py"], mesh.shape["px"]),
        mesh=mesh,
        in_specs=(P("py", "px", None), P("py", "px"), P("py", "px", None), P("py", "px", None)),
        out_specs=P("py", "px", None),
        check_vma=False,
    )
```

```python
import functools

import jax
import jax.numpy as jnp
from jax import lax
from jax.experimental import pallas as pl
from jax.experimental.pallas import tpu as pltpu
from jax.sharding import PartitionSpec as P

ITERS = 2
CHUNKS = 8
AHEAD = 2
LATE = 4
HALVES = 2
DIRECT = 0
PLAN = (("D", 0, 1), ("O", 4, 1), ("D", 1, 1), ("D", 2, 1), ("D", 3, 1), ("M", 4, 1), ("O", 5, 1), ("M", 5, 1), ("O", 6, 1), ("M", 6, 1), ("O", 7, 1), ("M", 7, 1))
MESH = pl.DeviceIdType.MESH
BF = jnp.bfloat16
F32 = jnp.float32


def split(x):
    hi = x.astype(BF)
    return hi, (x - hi.astype(F32)).astype(BF)


def mm(a, b):
    return lax.dot_general(a, b, (((1,), (0,)), ((), ())), preferred_element_type=F32)


def units_of(n_py, n_px, wid):
    if wid % 128 == 0 and n_px % 4 == 0 and n_py == 4:
        return PLAN
    return tuple(("D", c, 1) for c in range(CHUNKS))


def pieces_of(units, slots):
    pair = max(slots // 2, 1)
    early = len(units) - LATE
    pieces = [(u, 0, slots) for u in range(early)]
    return pieces + [(u, s, pair) for s in range(0, slots, pair) for u in range(early, len(units))]


def kernel(
    n_py, n_px, movie, traces, foot, ids, cur_out, scale_out,
    y_buf, outb, recv, land, crs, hilo, id_row, id_all, id_smem, t_send, t_recv, live_row, gram_buf,
    local_sem, own_sem, id_ssem, id_rsem, g_ssem, g_rsem, x_ssem, x_rsem, t_ssem, t_rsem, m_ssem, m_rsem,
    far_ids, far_smem, far_mat, far_ssem, far_rsem, *spans,
):
    py, px = lax.axis_index("py"), lax.axis_index("px")
    cur = cur_out
    total = n_py * n_px
    me = py * n_px + px
    loc, blk, wid = traces.shape
    nblk = loc * n_py
    slots = recv.shape[0]
    width = slots * blk
    direct = wid % 128 == 0
    pixels = y_buf.shape[0]
    step_rows = blk // CHUNKS
    units = units_of(n_py, n_px, wid)
    pieces = pieces_of(units, slots)
    pair = max(slots // 2, 1)
    nz = n_px // 2
    mirror = (nz - 1 - px // 2) * 2 + lax.rem(px, 2)
    side = n_px // 2
    base = (px // side) * side
    mine = pl.ds(py * loc, loc)
    across = [(py // 2) * 2 + 1 - lax.rem(py, 2), (1 - py // 2) * 2 + lax.rem(py, 2)]

    def rows_of(u):
        return pl.ds(units[u][1] * step_rows, units[u][2] * step_rows)

    barrier = pltpu.get_barrier_semaphore()

    def greet(device):
        pl.semaphore_signal(barrier, inc=1, device_id=device, device_id_type=MESH)

    def run(lo, hi, fn):
        def body(k, carry):
            fn(k)
            return carry

        lax.fori_loop(lo, hi, body, 0)

    run(1, n_px, lambda k: greet({"px": lax.rem(px + k, n_px)}))
    run(1, n_py, lambda k: greet({"py": lax.rem(py + k, n_py)}))

    owns = {
        u: pltpu.make_async_copy(traces.at[:, rows_of(u), :], spans[u].at[mine], own_sem.at[u])
        for u, unit in enumerate(units)
        if unit[0] != "M"
    }
    for own in owns.values():
        own.start()
    get_foot = pltpu.make_async_copy(foot, cur, local_sem.at[1])
    get_movie = pltpu.make_async_copy(movie, y_buf, local_sem.at[2])

    lane = lax.broadcasted_iota(jnp.int32, (1, 128), 1)
    row = jnp.zeros((1, 128), jnp.int32)
    for s in range(slots):
        row = jnp.where(lane == s, ids[0, 0, s], row)
    id_row[...] = row
    id_all[px] = row

    fill = jnp.zeros((slots, blk), jnp.int32)
    sub = lax.broadcasted_iota(jnp.int32, (slots, blk), 0)
    for s in range(slots):
        fill = jnp.where(sub == s, ids[0, 0, s], fill)
    for s in range(slots):
        alive = ((fill[s : s + 1, :] >= 0) & (fill[s : s + 1, :] < nblk)).astype(F32)
        live_row[:, s * blk : (s + 1) * blk] = alive
    pl.semaphore_wait(barrier, n_px - 1 + n_py - 1)

    def id_copy(k):
        return pltpu.make_async_remote_copy(
            src_ref=id_row, dst_ref=id_all.at[px], send_sem=id_ssem.at[k], recv_sem=id_rsem.at[k],
            device_id={"px": lax.rem(px + k, n_px)}, device_id_type=MESH,
        )

    def far_copy(k):
        dest = lax.rem(me + k, total)
        return pltpu.make_async_remote_copy(
            src_ref=id_row, dst_ref=far_ids.at[k - 1], send_sem=far_ssem.at[0], recv_sem=far_rsem.at[0],
            device_id={"py": dest // n_px, "px": lax.rem(dest, n_px)}, device_id_type=MESH,
        )

    def mirror_copy(u):
        return pltpu.make_async_remote_copy(
            src_ref=traces.at[:, rows_of(u), :], dst_ref=spans[u].at[mine],
            send_sem=m_ssem.at[u], recv_sem=m_rsem.at[u], device_id={"px": mirror}, device_id_type=MESH,
        )

    def held(u):
        return spans[u].at[mine] if units[u][0] == "M" else traces.at[:, rows_of(u), :]

    def gather_copy(u, k):
        return pltpu.make_async_remote_copy(
            src_ref=held(u), dst_ref=spans[u].at[mine], send_sem=g_ssem.at[u, k], recv_sem=g_rsem.at[u, k],
            device_id={"py": lax.rem(py + k, n_py)}, device_id_type=MESH,
        )

    def forwarded(u):
        return n_py == 4 and u >= DIRECT

    def near_copy(u, way):
        return pltpu.make_async_remote_copy(
            src_ref=held(u), dst_ref=spans[u].at[mine], send_sem=g_ssem.at[u, way], recv_sem=g_rsem.at[u, way],
            device_id={"py": across[way]}, device_id_type=MESH,
        )

    def far_half(u, way):
        part = spans[u].at[pl.ds(across[way] * loc + way * (loc // 2), loc // 2)]
        return pltpu.make_async_remote_copy(
            src_ref=part, dst_ref=part, send_sem=g_ssem.at[u, 2 + way], recv_sem=g_rsem.at[u, 2 + way],
            device_id={"py": across[1 - way]}, device_id_type=MESH,
        )

    def gather_start(u):
        if units[u][0] == "M":
            mirror_copy(u).wait_recv()
        if forwarded(u):
            for way in range(2):
                near_copy(u, way).start()
        else:
            run(1, n_py, lambda k: gather_copy(u, k).start())

    def gather_turn(u):
        if forwarded(u):
            for way in range(2):
                near_copy(u, way).wait_recv()
                far_half(u, way).start()

    def gather_end(u):
        if forwarded(u):
            for way in range(2):
                far_half(u, way).wait_recv()
        else:
            run(1, n_py, lambda k: gather_copy(u, k).wait_recv())
        if units[u][0] != "M":
            owns[u].wait()

    def gather_sent(u):
        if forwarded(u):
            for way in range(2):
                near_copy(u, way).wait_send()
                far_half(u, way).wait_send()
        else:
            run(1, n_py, lambda k: gather_copy(u, k).wait_send())

    def reach(u):
        return n_px if units[u][0] == "D" else side

    def x_dest(u, k):
        return lax.rem(px + k, n_px) if units[u][0] == "D" else base + lax.rem(px - base + k, side)

    def staged(u, dest):
        return n_px - 1 - dest if units[u][0] == "M" else dest

    def frames_at(u):
        source = mirror if units[u][0] == "M" else px
        return pl.ds(pl.multiple_of(source * wid, wid), wid)

    def x_copy(c, k):
        u, low, many = pieces[c]
        rows = rows_of(u)
        group = pl.ds(low, many)
        dest = x_dest(u, k)
        target = recv.at[group, rows, frames_at(u)] if direct else land.at[px, group, rows, :]
        return pltpu.make_async_remote_copy(
            src_ref=outb.at[staged(u, dest), group, rows, :],
            dst_ref=target,
            send_sem=x_ssem.at[c, k], recv_sem=x_rsem.at[c, k],
            device_id={"px": dest}, device_id_type=MESH,
        )

    run(1, n_px, lambda k: id_copy(k).start())
    for u in range(AHEAD):
        if u == AHEAD - 1:
            for v, unit in enumerate(units):
                if unit[0] == "M":
                    mirror_copy(v).start()
        gather_start(u)
    get_movie.start()
    get_foot.start()
    run(1, n_px, lambda k: id_copy(k).wait())
    to_smem = pltpu.make_async_copy(id_all, id_smem, local_sem.at[3])
    to_smem.start()
    to_smem.wait()

    def pick(dest, s, u):
        number = id_smem[dest, 0, s]
        ok = ((number >= 0) & (number < nblk)).astype(F32).astype(BF)
        index = jnp.minimum(jnp.maximum(number, 0), nblk - 1)
        return spans[u][index] * ok

    def deal(c):
        u, low, many = pieces[c]
        rows = rows_of(u)

        def route(k):
            dest = x_dest(u, k)
            for s in range(low, low + many):
                outb[staged(u, dest), s, rows, :] = pick(dest, s, u)
            x_copy(c, k).start()

        run(1, reach(u), route)
        for s in range(low, low + many):
            if direct:
                recv[s, rows, frames_at(u)] = pick(px, s, u)
            else:
                land[px, s, rows, :] = pick(px, s, u)

    for u in range(len(units) + 1):
        if u < len(units):
            gather_turn(u)
            if u + AHEAD < len(units):
                gather_start(u + AHEAD)
        if u:
            gather_end(u - 1)
            deal(u - 1)
        if u == 2:
            run(1, total, lambda k: far_copy(k).start())
    for c in range(len(units), len(pieces)):
        deal(c)

    pltpu.make_async_copy(far_ids, far_ids, far_rsem.at[0]).wait()
    to_far = pltpu.make_async_copy(far_ids, far_smem, local_sem.at[7])
    to_far.start()
    get_foot.wait()
    get_movie.wait()
    live = live_row[...]
    part = min(pixels, 512)
    frames = recv.shape[2]

    def cross_part(low, i):
        at = pl.ds(pl.multiple_of(i * part, part), part)
        cols = pl.ds(low * blk, pair * blk)
        crs[at, cols] = lax.dot_general(
            y_buf[at, :], recv[low : low + pair].reshape(pair * blk, frames), (((1,), (1,)), ((), ())),
            preferred_element_type=F32,
        )

    def age(i):
        at = pl.ds(pl.multiple_of(i * part, part), part)
        cur[at, :] = cur[at, :] * live

    run(0, pixels // part, age)
    to_far.wait()

    def spread(k):
        mat = jnp.zeros((slots, blk), jnp.int32)
        for s in range(slots):
            mat = jnp.where(sub == s, far_smem[k, 0, s], mat)
        far_mat[k] = mat

    run(0, total - 1, spread)
    for c, (u, low, many) in enumerate(pieces):
        run(1, reach(u), lambda k: x_copy(c, k).wait_recv())
        if many == slots > 1 or u < len(units) - 1:
            continue
        if not direct:
            pack = 128 // wid
            for q in range(n_px // pack):
                both = [land[q * pack + j, low : low + many] for j in range(pack)]
                recv[low : low + many, :, q * 128 : (q + 1) * 128] = jnp.concatenate(both, axis=-1)
        run(0, pixels // part, lambda i: cross_part(low, i))
        near = slice(low * blk, (low + many) * blk)
        far = slice(0, (low + many) * blk)
        fresh_rows = lax.dot_general(
            recv[low : low + many].reshape(many * blk, frames), recv[: low + many].reshape((low + many) * blk, frames),
            (((1,), (1,)), ((), ())), preferred_element_type=F32,
        )
        gram_buf[near, far] = fresh_rows
        if low:
            gram_buf[: low * blk, near] = fresh_rows[:, : low * blk].T

    gram = gram_buf[...]
    eye = lax.broadcasted_iota(jnp.int32, (width, width), 0) == lax.broadcasted_iota(jnp.int32, (width, width), 1)
    denom = jnp.sum(jnp.where(eye, gram, 0.0), axis=0, keepdims=True) + 1e-06 + (1.0 - live)
    inv = 1.0 / denom
    hi, lo = split(jnp.where(eye, 1.0, 0.0) - gram * inv)
    for s in range(slots):
        hilo[s, :, :blk] = hi[:, s * blk : (s + 1) * blk]
        hilo[s, :, blk:] = lo[:, s * blk : (s + 1) * blk]
    def total_copy(step, k):
        dest = lax.rem(me + k, total)
        return pltpu.make_async_remote_copy(
            src_ref=t_send.at[step], dst_ref=t_recv.at[step, k - 1],
            send_sem=t_ssem.at[step], recv_sem=t_rsem.at[step],
            device_id={"py": dest // n_px, "px": lax.rem(dest, n_px)}, device_id_type=MESH,
        )

    scale = jnp.ones((1, width), F32)
    for step in range(ITERS):

        def sweep(i, sums, scale=scale):
            ats = [pl.ds(pl.multiple_of(i * whole + h * half_rows, half_rows), half_rows) for h in range(HALVES)]
            his, los = [], []
            for at in ats:
                now = cur[at, :] if step == 0 else cur[at, :] * scale
                both = [split(now[:, s * blk : (s + 1) * blk]) for s in range(slots)]
                his.append([b[0] for b in both])
                los.append([b[1] for b in both])
            squares = []
            for s in range(slots):
                m = hilo[s]
                low = slice(s * blk, (s + 1) * blk)
                prods = []
                for h in range(HALVES):
                    wide = mm(jnp.concatenate(his[h], axis=1), m)
                    thin = mm(jnp.concatenate(los[h], axis=1), m[:, :blk])
                    prods.append(wide[:, :blk] + wide[:, blk:] + thin)
                square = jnp.zeros((1, blk), F32)
                for h, at in enumerate(ats):
                    fresh = jnp.maximum(crs[at, low] * inv[:, low] + prods[h], 0.0)
                    cur[at, low] = fresh
                    his[h][s], los[h][s] = split(fresh)
                    square = square + jnp.sum(fresh * fresh, axis=0, keepdims=True)
                squares.append(square)
            return sums + jnp.concatenate(squares, axis=1)

        whole = min(pixels, 1024)
        half_rows = whole // HALVES
        sums = lax.fori_loop(0, pixels // whole, sweep, jnp.zeros((1, width), F32))
        for s in range(slots):
            t_send[step, s : s + 1, :] = sums[:, s * blk : (s + 1) * blk]
        run(1, total, lambda k: total_copy(step, k).start())
        if step == 0:
            for u, unit in enumerate(units):
                gather_sent(u)
                if unit[0] == "M":
                    mirror_copy(u).wait_send()
            for c, (u, low, many) in enumerate(pieces):
                run(1, reach(u), lambda k: x_copy(c, k).wait_send())
            pltpu.make_async_copy(far_ids, far_ids, far_ssem.at[0]).wait()
        pltpu.make_async_copy(t_recv.at[step], t_recv.at[step], t_rsem.at[step]).wait()
        got = t_recv[step]
        scales = []
        for s in range(slots):
            acc = sums[:, s * blk : (s + 1) * blk]
            same = jnp.where(far_mat[...] == ids[0, 0, s], got, 0.0)
            acc = acc + jnp.sum(jnp.sum(same, axis=0), axis=0, keepdims=True)
            scales.append(1.0 / jnp.sqrt(acc / (pixels * total) + 1e-06))
        scale = jnp.concatenate(scales, axis=1) * live
    scale_out[...] = scale

    for step in range(ITERS):
        pltpu.make_async_copy(t_recv.at[step], t_recv.at[step], t_ssem.at[step]).wait()


def per_device(n_py, n_px, movie, traces, footprints, block_ids):
    rows, cols, frames = movie.shape
    pixels = rows * cols
    width = footprints.shape[-1]
    slots = block_ids.shape[-1]
    blk = width // slots
    wid = traces.shape[1]
    loc = traces.shape[0] // blk
    total = n_py * n_px
    units = units_of(n_py, n_px, wid)
    pieces = pieces_of(units, slots)
    hbm = pl.BlockSpec(memory_space=pltpu.VMEM)
    dma = pltpu.SemaphoreType.DMA
    current, scale = pl.pallas_call(
        functools.partial(kernel, n_py, n_px),
        out_shape=(
            jax.ShapeDtypeStruct((pixels, width), F32),
            jax.ShapeDtypeStruct((1, width), F32),
        ),
        in_specs=[pl.BlockSpec(memory_space=pltpu.HBM)] * 3 + [pl.BlockSpec(memory_space=pltpu.SMEM)],
        out_specs=(hbm, pl.BlockSpec(memory_space=pltpu.VMEM)),
        scratch_shapes=[
            pltpu.VMEM((pixels, frames), BF),
            pltpu.VMEM((n_px, slots, blk, wid), BF),
            pltpu.VMEM((slots, blk, frames), BF),
            pltpu.VMEM((8, 128) if wid % 128 == 0 else (n_px, slots, blk, wid), BF),
            pltpu.VMEM((pixels, width), F32),
            pltpu.VMEM((slots, width, 2 * blk), BF),
            pltpu.VMEM((1, 128), jnp.int32),
            pltpu.VMEM((n_px, 1, 128), jnp.int32),
            pltpu.SMEM((n_px, 1, 128), jnp.int32),
            pltpu.VMEM((ITERS, slots, blk), F32),
            pltpu.VMEM((ITERS, total - 1, slots, blk), F32),
            pltpu.VMEM((1, width), F32),
            pltpu.VMEM((width, width), F32),
            dma((8,)), dma((len(units),)),
            dma((n_px,)), dma((n_px,)),
            dma((len(units), n_py)), dma((len(units), n_py)),
            dma((len(pieces), n_px)), dma((len(pieces), n_px)),
            dma((ITERS,)), dma((ITERS,)),
            dma((len(units),)), dma((len(units),)),
            pltpu.VMEM((total - 1, 1, 128), jnp.int32),
            pltpu.SMEM((total - 1, 1, 128), jnp.int32),
            pltpu.VMEM((total - 1, slots, blk), jnp.int32),
            dma((1,)), dma((1,)),
            *[pltpu.VMEM((loc * n_py, unit[2] * (blk // CHUNKS), wid), BF) for unit in units],
        ],
        compiler_params=pltpu.CompilerParams(
            collective_id=0, has_side_effects=True, vmem_limit_bytes=28 * 2**20
        ),
    )(
        pltpu.with_memory_space_constraint(movie.reshape(pixels, frames), pltpu.HBM),
        pltpu.with_memory_space_constraint(traces.reshape(loc, blk, wid), pltpu.HBM),
        pltpu.with_memory_space_constraint(footprints.reshape(pixels, width), pltpu.HBM),
        pltpu.with_memory_space_constraint(block_ids, pltpu.HBM),
    )
    return (current * scale).reshape(rows, cols, width)


def solution(mesh):
    return jax.shard_map(
        functools.partial(per_device, mesh.shape["py"], mesh.shape["px"]),
        mesh=mesh,
        in_specs=(P("py", "px", None), P("py", "px"), P("py", "px", None), P("py", "px", None)),
        out_specs=P("py", "px", None),
        check_vma=False,
    )
```

```python
import functools

import jax
import jax.numpy as jnp
from jax import lax
from jax.experimental import pallas as pl
from jax.experimental.pallas import tpu as pltpu
from jax.sharding import PartitionSpec as P

ITERS = 2
CHUNKS = 8
AHEAD = 2
LATE = 4
HALVES = 2
DIRECT = 0
PLAN = (("D", 0, 1), ("O", 4, 1), ("D", 1, 1), ("D", 2, 1), ("D", 3, 1), ("M", 4, 1), ("O", 5, 1), ("M", 5, 1), ("O", 6, 1), ("M", 6, 1), ("O", 7, 1), ("M", 7, 1))
MESH = pl.DeviceIdType.MESH
BF = jnp.bfloat16
F32 = jnp.float32


def split(x):
    hi = x.astype(BF)
    return hi, (x - hi.astype(F32)).astype(BF)


def mm(a, b):
    return lax.dot_general(a, b, (((1,), (0,)), ((), ())), preferred_element_type=F32)


def units_of(n_py, n_px, wid):
    if wid % 128 == 0 and n_px % 4 == 0 and n_py == 4:
        return PLAN
    return tuple(("D", c, 1) for c in range(CHUNKS))


def pieces_of(units, slots):
    pair = max(slots // 2, 1)
    early = len(units) - LATE
    pieces = [(u, 0, slots) for u in range(early)]
    return pieces + [(u, s, pair) for s in range(0, slots, pair) for u in range(early, len(units))]


def kernel(
    n_py, n_px, movie, traces, foot, ids, cur_out, scale_out,
    y_buf, outb, recv, land, crs, hilo, id_row, id_all, id_smem, t_send, t_recv, live_row, gram_buf,
    local_sem, own_sem, id_ssem, id_rsem, g_ssem, g_rsem, x_ssem, x_rsem, t_ssem, t_rsem, m_ssem, m_rsem,
    far_ids, far_smem, far_mat, far_ssem, far_rsem, *spans,
):
    py, px = lax.axis_index("py"), lax.axis_index("px")
    cur = cur_out
    total = n_py * n_px
    me = py * n_px + px
    loc, blk, wid = traces.shape
    nblk = loc * n_py
    slots = recv.shape[0]
    width = slots * blk
    direct = wid % 128 == 0
    pixels = y_buf.shape[0]
    step_rows = blk // CHUNKS
    units = units_of(n_py, n_px, wid)
    pieces = pieces_of(units, slots)
    pair = max(slots // 2, 1)
    nz = n_px // 2
    mirror = (nz - 1 - px // 2) * 2 + lax.rem(px, 2)
    side = n_px // 2
    base = (px // side) * side
    mine = pl.ds(py * loc, loc)
    across = [(py // 2) * 2 + 1 - lax.rem(py, 2), (1 - py // 2) * 2 + lax.rem(py, 2)]

    def rows_of(u):
        return pl.ds(units[u][1] * step_rows, units[u][2] * step_rows)

    barrier = pltpu.get_barrier_semaphore()

    def greet(device):
        pl.semaphore_signal(barrier, inc=1, device_id=device, device_id_type=MESH)

    def run(lo, hi, fn):
        def body(k, carry):
            fn(k)
            return carry

        lax.fori_loop(lo, hi, body, 0)

    run(1, n_px, lambda k: greet({"px": lax.rem(px + k, n_px)}))
    run(1, n_py, lambda k: greet({"py": lax.rem(py + k, n_py)}))

    owns = {
        u: pltpu.make_async_copy(traces.at[:, rows_of(u), :], spans[u].at[mine], own_sem.at[u])
        for u, unit in enumerate(units)
        if unit[0] != "M"
    }
    for own in owns.values():
        own.start()
    get_foot = pltpu.make_async_copy(foot, cur, local_sem.at[1])
    get_movie = pltpu.make_async_copy(movie, y_buf, local_sem.at[2])

    lane = lax.broadcasted_iota(jnp.int32, (1, 128), 1)
    row = jnp.zeros((1, 128), jnp.int32)
    for s in range(slots):
        row = jnp.where(lane == s, ids[0, 0, s], row)
    id_row[...] = row
    id_all[px] = row

    fill = jnp.zeros((slots, blk), jnp.int32)
    sub = lax.broadcasted_iota(jnp.int32, (slots, blk), 0)
    for s in range(slots):
        fill = jnp.where(sub == s, ids[0, 0, s], fill)
    for s in range(slots):
        alive = ((fill[s : s + 1, :] >= 0) & (fill[s : s + 1, :] < nblk)).astype(F32)
        live_row[:, s * blk : (s + 1) * blk] = alive
    pl.semaphore_wait(barrier, n_px - 1 + n_py - 1)

    def id_copy(k):
        return pltpu.make_async_remote_copy(
            src_ref=id_row, dst_ref=id_all.at[px], send_sem=id_ssem.at[k], recv_sem=id_rsem.at[k],
            device_id={"px": lax.rem(px + k, n_px)}, device_id_type=MESH,
        )

    def far_copy(k):
        dest = lax.rem(me + k, total)
        return pltpu.make_async_remote_copy(
            src_ref=id_row, dst_ref=far_ids.at[k - 1], send_sem=far_ssem.at[0], recv_sem=far_rsem.at[0],
            device_id={"py": dest // n_px, "px": lax.rem(dest, n_px)}, device_id_type=MESH,
        )

    def mirror_copy(u):
        return pltpu.make_async_remote_copy(
            src_ref=traces.at[:, rows_of(u), :], dst_ref=spans[u].at[mine],
            send_sem=m_ssem.at[u], recv_sem=m_rsem.at[u], device_id={"px": mirror}, device_id_type=MESH,
        )

    def held(u):
        return spans[u].at[mine] if units[u][0] == "M" else traces.at[:, rows_of(u), :]

    def gather_copy(u, k):
        return pltpu.make_async_remote_copy(
            src_ref=held(u), dst_ref=spans[u].at[mine], send_sem=g_ssem.at[u, k], recv_sem=g_rsem.at[u, k],
            device_id={"py": lax.rem(py + k, n_py)}, device_id_type=MESH,
        )

    def forwarded(u):
        return n_py == 4 and u >= DIRECT

    def near_copy(u, way):
        return pltpu.make_async_remote_copy(
            src_ref=held(u), dst_ref=spans[u].at[mine], send_sem=g_ssem.at[u, way], recv_sem=g_rsem.at[u, way],
            device_id={"py": across[way]}, device_id_type=MESH,
        )

    def far_half(u, way):
        part = spans[u].at[pl.ds(across[way] * loc + way * (loc // 2), loc // 2)]
        return pltpu.make_async_remote_copy(
            src_ref=part, dst_ref=part, send_sem=g_ssem.at[u, 2 + way], recv_sem=g_rsem.at[u, 2 + way],
            device_id={"py": across[1 - way]}, device_id_type=MESH,
        )

    def gather_start(u):
        if units[u][0] == "M":
            mirror_copy(u).wait_recv()
        if forwarded(u):
            for way in range(2):
                near_copy(u, way).start()
        else:
            run(1, n_py, lambda k: gather_copy(u, k).start())

    def gather_turn(u):
        if forwarded(u):
            for way in range(2):
                near_copy(u, way).wait_recv()
                far_half(u, way).start()

    def gather_end(u):
        if forwarded(u):
            for way in range(2):
                far_half(u, way).wait_recv()
        else:
            run(1, n_py, lambda k: gather_copy(u, k).wait_recv())
        if units[u][0] != "M":
            owns[u].wait()

    def gather_sent(u):
        if forwarded(u):
            for way in range(2):
                near_copy(u, way).wait_send()
                far_half(u, way).wait_send()
        else:
            run(1, n_py, lambda k: gather_copy(u, k).wait_send())

    def reach(u):
        return n_px if units[u][0] == "D" else side

    def x_dest(u, k):
        return lax.rem(px + k, n_px) if units[u][0] == "D" else base + lax.rem(px - base + k, side)

    def staged(u, dest):
        return n_px - 1 - dest if units[u][0] == "M" else dest

    def frames_at(u):
        source = mirror if units[u][0] == "M" else px
        return pl.ds(pl.multiple_of(source * wid, wid), wid)

    def x_copy(c, k):
        u, low, many = pieces[c]
        rows = rows_of(u)
        group = pl.ds(low, many)
        dest = x_dest(u, k)
        target = recv.at[group, rows, frames_at(u)] if direct else land.at[px, group, rows, :]
        return pltpu.make_async_remote_copy(
            src_ref=outb.at[staged(u, dest), group, rows, :],
            dst_ref=target,
            send_sem=x_ssem.at[c, k], recv_sem=x_rsem.at[c, k],
            device_id={"px": dest}, device_id_type=MESH,
        )

    run(1, n_px, lambda k: id_copy(k).start())
    for u in range(AHEAD):
        if u == AHEAD - 1:
            for v, unit in enumerate(units):
                if unit[0] == "M":
                    mirror_copy(v).start()
        gather_start(u)
    get_movie.start()
    get_foot.start()
    run(1, n_px, lambda k: id_copy(k).wait())
    to_smem = pltpu.make_async_copy(id_all, id_smem, local_sem.at[3])
    to_smem.start()
    to_smem.wait()

    def pick(dest, s, u):
        number = id_smem[dest, 0, s]
        ok = ((number >= 0) & (number < nblk)).astype(F32).astype(BF)
        index = jnp.minimum(jnp.maximum(number, 0), nblk - 1)
        return spans[u][index] * ok

    def deal(c):
        u, low, many = pieces[c]
        rows = rows_of(u)

        def route(k):
            dest = x_dest(u, k)
            for s in range(low, low + many):
                outb[staged(u, dest), s, rows, :] = pick(dest, s, u)
            x_copy(c, k).start()

        run(1, reach(u), route)
        for s in range(low, low + many):
            if direct:
                recv[s, rows, frames_at(u)] = pick(px, s, u)
            else:
                land[px, s, rows, :] = pick(px, s, u)

    for u in range(len(units) + 1):
        if u < len(units):
            gather_turn(u)
            if u + AHEAD < len(units):
                gather_start(u + AHEAD)
        if u:
            gather_end(u - 1)
            deal(u - 1)
        if u == 2:
            run(1, total, lambda k: far_copy(k).start())
    for c in range(len(units), len(pieces)):
        deal(c)

    pltpu.make_async_copy(far_ids, far_ids, far_rsem.at[0]).wait()
    to_far = pltpu.make_async_copy(far_ids, far_smem, local_sem.at[7])
    to_far.start()
    get_foot.wait()
    get_movie.wait()
    live = live_row[...]
    part = min(pixels, 512)
    frames = recv.shape[2]

    def cross_part(low, i):
        at = pl.ds(pl.multiple_of(i * part, part), part)
        cols = pl.ds(low * blk, pair * blk)
        crs[at, cols] = lax.dot_general(
            y_buf[at, :], recv[low : low + pair].reshape(pair * blk, frames), (((1,), (1,)), ((), ())),
            preferred_element_type=F32,
        )

    def age(i):
        at = pl.ds(pl.multiple_of(i * part, part), part)
        cur[at, :] = cur[at, :] * live

    run(0, pixels // part, age)
    to_far.wait()

    def spread(k):
        mat = jnp.zeros((slots, blk), jnp.int32)
        for s in range(slots):
            mat = jnp.where(sub == s, far_smem[k, 0, s], mat)
        far_mat[k] = mat

    run(0, total - 1, spread)
    for c, (u, low, many) in enumerate(pieces):
        run(1, reach(u), lambda k: x_copy(c, k).wait_recv())
        if many == slots > 1 or u < len(units) - 1:
            continue
        if not direct:
            pack = 128 // wid
            for q in range(n_px // pack):
                both = [land[q * pack + j, low : low + many] for j in range(pack)]
                recv[low : low + many, :, q * 128 : (q + 1) * 128] = jnp.concatenate(both, axis=-1)
        run(0, pixels // part, lambda i: cross_part(low, i))
        near = slice(low * blk, (low + many) * blk)
        far = slice(0, (low + many) * blk)
        fresh_rows = lax.dot_general(
            recv[low : low + many].reshape(many * blk, frames), recv[: low + many].reshape((low + many) * blk, frames),
            (((1,), (1,)), ((), ())), preferred_element_type=F32,
        )
        gram_buf[near, far] = fresh_rows
        if low:
            gram_buf[: low * blk, near] = fresh_rows[:, : low * blk].T

    gram = gram_buf[...]
    eye = lax.broadcasted_iota(jnp.int32, (width, width), 0) == lax.broadcasted_iota(jnp.int32, (width, width), 1)
    denom = jnp.sum(jnp.where(eye, gram, 0.0), axis=0, keepdims=True) + 1e-06 + (1.0 - live)
    inv = 1.0 / denom
    hi, lo = split(jnp.where(eye, 1.0, 0.0) - gram * inv)
    for s in range(slots):
        hilo[s, :, :blk] = hi[:, s * blk : (s + 1) * blk]
        hilo[s, :, blk:] = lo[:, s * blk : (s + 1) * blk]
    def total_copy(step, k):
        dest = lax.rem(me + k, total)
        return pltpu.make_async_remote_copy(
            src_ref=t_send.at[step], dst_ref=t_recv.at[step, k - 1],
            send_sem=t_ssem.at[step], recv_sem=t_rsem.at[step],
            device_id={"py": dest // n_px, "px": lax.rem(dest, n_px)}, device_id_type=MESH,
        )

    def total_start(step):
        if n_py != 4:
            run(1, total, lambda k: total_copy(step, k).start())
            return
        upper = px // side
        for row in (n_py - 1 - py, across[0], across[1], py):

            def one(j):
                dest = row * n_px + (1 - upper) * (n_px - 1 - j) + upper * j
                k = lax.rem(dest - me + total, total)
                if row is py:
                    pl.when(k > 0)(lambda: total_copy(step, k).start())
                else:
                    total_copy(step, k).start()

            for j in range(n_px):
                one(j)

    scale = jnp.ones((1, width), F32)
    for step in range(ITERS):

        def sweep(i, sums, scale=scale):
            ats = [pl.ds(pl.multiple_of(i * whole + h * half_rows, half_rows), half_rows) for h in range(HALVES)]
            his, los = [], []
            for at in ats:
                now = cur[at, :] if step == 0 else cur[at, :] * scale
                both = [split(now[:, s * blk : (s + 1) * blk]) for s in range(slots)]
                his.append([b[0] for b in both])
                los.append([b[1] for b in both])
            squares = []
            for s in range(slots):
                m = hilo[s]
                low = slice(s * blk, (s + 1) * blk)
                prods = []
                for h in range(HALVES):
                    wide = mm(jnp.concatenate(his[h], axis=1), m)
                    thin = mm(jnp.concatenate(los[h], axis=1), m[:, :blk])
                    prods.append(wide[:, :blk] + wide[:, blk:] + thin)
                square = jnp.zeros((1, blk), F32)
                for h, at in enumerate(ats):
                    fresh = jnp.maximum(crs[at, low] * inv[:, low] + prods[h], 0.0)
                    cur[at, low] = fresh
                    his[h][s], los[h][s] = split(fresh)
                    square = square + jnp.sum(fresh * fresh, axis=0, keepdims=True)
                squares.append(square)
            return sums + jnp.concatenate(squares, axis=1)

        whole = min(pixels, 1024)
        half_rows = whole // HALVES
        sums = lax.fori_loop(0, pixels // whole, sweep, jnp.zeros((1, width), F32))
        for s in range(slots):
            t_send[step, s : s + 1, :] = sums[:, s * blk : (s + 1) * blk]
        total_start(step)
        if step == 0:
            for u, unit in enumerate(units):
                gather_sent(u)
                if unit[0] == "M":
                    mirror_copy(u).wait_send()
            for c, (u, low, many) in enumerate(pieces):
                run(1, reach(u), lambda k: x_copy(c, k).wait_send())
            pltpu.make_async_copy(far_ids, far_ids, far_ssem.at[0]).wait()
        pltpu.make_async_copy(t_recv.at[step], t_recv.at[step], t_rsem.at[step]).wait()
        got = t_recv[step]
        scales = []
        for s in range(slots):
            acc = sums[:, s * blk : (s + 1) * blk]
            same = jnp.where(far_mat[...] == ids[0, 0, s], got, 0.0)
            acc = acc + jnp.sum(jnp.sum(same, axis=0), axis=0, keepdims=True)
            scales.append(1.0 / jnp.sqrt(acc / (pixels * total) + 1e-06))
        scale = jnp.concatenate(scales, axis=1) * live
    scale_out[...] = scale

    for step in range(ITERS):
        pltpu.make_async_copy(t_recv.at[step], t_recv.at[step], t_ssem.at[step]).wait()


def per_device(n_py, n_px, movie, traces, footprints, block_ids):
    rows, cols, frames = movie.shape
    pixels = rows * cols
    width = footprints.shape[-1]
    slots = block_ids.shape[-1]
    blk = width // slots
    wid = traces.shape[1]
    loc = traces.shape[0] // blk
    total = n_py * n_px
    units = units_of(n_py, n_px, wid)
    pieces = pieces_of(units, slots)
    hbm = pl.BlockSpec(memory_space=pltpu.VMEM)
    dma = pltpu.SemaphoreType.DMA
    current, scale = pl.pallas_call(
        functools.partial(kernel, n_py, n_px),
        out_shape=(
            jax.ShapeDtypeStruct((pixels, width), F32),
            jax.ShapeDtypeStruct((1, width), F32),
        ),
        in_specs=[pl.BlockSpec(memory_space=pltpu.HBM)] * 3 + [pl.BlockSpec(memory_space=pltpu.SMEM)],
        out_specs=(hbm, pl.BlockSpec(memory_space=pltpu.VMEM)),
        scratch_shapes=[
            pltpu.VMEM((pixels, frames), BF),
            pltpu.VMEM((n_px, slots, blk, wid), BF),
            pltpu.VMEM((slots, blk, frames), BF),
            pltpu.VMEM((8, 128) if wid % 128 == 0 else (n_px, slots, blk, wid), BF),
            pltpu.VMEM((pixels, width), F32),
            pltpu.VMEM((slots, width, 2 * blk), BF),
            pltpu.VMEM((1, 128), jnp.int32),
            pltpu.VMEM((n_px, 1, 128), jnp.int32),
            pltpu.SMEM((n_px, 1, 128), jnp.int32),
            pltpu.VMEM((ITERS, slots, blk), F32),
            pltpu.VMEM((ITERS, total - 1, slots, blk), F32),
            pltpu.VMEM((1, width), F32),
            pltpu.VMEM((width, width), F32),
            dma((8,)), dma((len(units),)),
            dma((n_px,)), dma((n_px,)),
            dma((len(units), n_py)), dma((len(units), n_py)),
            dma((len(pieces), n_px)), dma((len(pieces), n_px)),
            dma((ITERS,)), dma((ITERS,)),
            dma((len(units),)), dma((len(units),)),
            pltpu.VMEM((total - 1, 1, 128), jnp.int32),
            pltpu.SMEM((total - 1, 1, 128), jnp.int32),
            pltpu.VMEM((total - 1, slots, blk), jnp.int32),
            dma((1,)), dma((1,)),
            *[pltpu.VMEM((loc * n_py, unit[2] * (blk // CHUNKS), wid), BF) for unit in units],
        ],
        compiler_params=pltpu.CompilerParams(
            collective_id=0, has_side_effects=True, vmem_limit_bytes=28 * 2**20
        ),
    )(
        pltpu.with_memory_space_constraint(movie.reshape(pixels, frames), pltpu.HBM),
        pltpu.with_memory_space_constraint(traces.reshape(loc, blk, wid), pltpu.HBM),
        pltpu.with_memory_space_constraint(footprints.reshape(pixels, width), pltpu.HBM),
        pltpu.with_memory_space_constraint(block_ids, pltpu.HBM),
    )
    return (current * scale).reshape(rows, cols, width)


def solution(mesh):
    return jax.shard_map(
        functools.partial(per_device, mesh.shape["py"], mesh.shape["px"]),
        mesh=mesh,
        in_specs=(P("py", "px", None), P("py", "px"), P("py", "px", None), P("py", "px", None)),
        out_specs=P("py", "px", None),
        check_vma=False,
    )
```

```python
import functools

import jax
import jax.numpy as jnp
from jax import lax
from jax.experimental import pallas as pl
from jax.experimental.pallas import tpu as pltpu
from jax.sharding import PartitionSpec as P

ITERS = 2
CHUNKS = 8
AHEAD = 2
LATE = 4
HALVES = 2
DIRECT = 0
PLAN = (("D", 0, 1), ("O", 4, 1), ("D", 1, 1), ("D", 2, 1), ("D", 3, 1), ("M", 4, 1), ("O", 5, 1), ("M", 5, 1), ("O", 6, 1), ("M", 6, 1), ("O", 7, 1), ("M", 7, 1))
MESH = pl.DeviceIdType.MESH
BF = jnp.bfloat16
F32 = jnp.float32


def split(x):
    hi = x.astype(BF)
    return hi, (x - hi.astype(F32)).astype(BF)


def mm(a, b):
    return lax.dot_general(a, b, (((1,), (0,)), ((), ())), preferred_element_type=F32)


def units_of(n_py, n_px, wid):
    if wid % 128 == 0 and n_px % 4 == 0 and n_py == 4:
        return PLAN
    return tuple(("D", c, 1) for c in range(CHUNKS))


def pieces_of(units, slots):
    pair = max(slots // 2, 1)
    early = len(units) - LATE
    pieces = [(u, 0, slots) for u in range(early)]
    return pieces + [(u, s, pair) for s in range(0, slots, pair) for u in range(early, len(units))]


def kernel(
    n_py, n_px, movie, traces, foot, ids, cur_out, scale_out,
    y_buf, outb, recv, land, crs, hilo, id_row, id_all, id_smem, t_send, t_recv, live_row, gram_buf,
    local_sem, own_sem, id_ssem, id_rsem, g_ssem, g_rsem, x_ssem, x_rsem, t_ssem, t_rsem, m_ssem, m_rsem,
    far_ids, far_smem, far_mat, far_ssem, far_rsem, *spans,
):
    py, px = lax.axis_index("py"), lax.axis_index("px")
    cur = cur_out
    total = n_py * n_px
    me = py * n_px + px
    loc, blk, wid = traces.shape
    nblk = loc * n_py
    slots = recv.shape[0]
    width = slots * blk
    direct = wid % 128 == 0
    pixels = y_buf.shape[0]
    step_rows = blk // CHUNKS
    units = units_of(n_py, n_px, wid)
    pieces = pieces_of(units, slots)
    pair = max(slots // 2, 1)
    nz = n_px // 2
    mirror = (nz - 1 - px // 2) * 2 + lax.rem(px, 2)
    side = n_px // 2
    base = (px // side) * side
    mine = pl.ds(py * loc, loc)
    across = [(py // 2) * 2 + 1 - lax.rem(py, 2), (1 - py // 2) * 2 + lax.rem(py, 2)]

    def rows_of(u):
        return pl.ds(units[u][1] * step_rows, units[u][2] * step_rows)

    barrier = pltpu.get_barrier_semaphore()

    def greet(device):
        pl.semaphore_signal(barrier, inc=1, device_id=device, device_id_type=MESH)

    def run(lo, hi, fn):
        def body(k, carry):
            fn(k)
            return carry

        lax.fori_loop(lo, hi, body, 0)

    for k in range(1, n_px):
        greet({"px": lax.rem(px + k, n_px)})
    for k in range(1, n_py):
        greet({"py": lax.rem(py + k, n_py)})

    owns = {
        u: pltpu.make_async_copy(traces.at[:, rows_of(u), :], spans[u].at[mine], own_sem.at[u])
        for u, unit in enumerate(units)
        if unit[0] != "M"
    }
    for own in owns.values():
        own.start()
    get_foot = pltpu.make_async_copy(foot, cur, local_sem.at[1])
    get_movie = pltpu.make_async_copy(movie, y_buf, local_sem.at[2])

    lane = lax.broadcasted_iota(jnp.int32, (1, 128), 1)
    row = jnp.zeros((1, 128), jnp.int32)
    for s in range(slots):
        row = jnp.where(lane == s, ids[0, 0, s], row)
    id_row[...] = row
    id_all[px] = row

    fill = jnp.zeros((slots, blk), jnp.int32)
    sub = lax.broadcasted_iota(jnp.int32, (slots, blk), 0)
    for s in range(slots):
        fill = jnp.where(sub == s, ids[0, 0, s], fill)
    for s in range(slots):
        alive = ((fill[s : s + 1, :] >= 0) & (fill[s : s + 1, :] < nblk)).astype(F32)
        live_row[:, s * blk : (s + 1) * blk] = alive
    pl.semaphore_wait(barrier, n_px - 1 + n_py - 1)

    def id_copy(k):
        return pltpu.make_async_remote_copy(
            src_ref=id_row, dst_ref=id_all.at[px], send_sem=id_ssem.at[k], recv_sem=id_rsem.at[k],
            device_id={"px": lax.rem(px + k, n_px)}, device_id_type=MESH,
        )

    def far_copy(k):
        dest = lax.rem(me + k, total)
        return pltpu.make_async_remote_copy(
            src_ref=id_row, dst_ref=far_ids.at[k - 1], send_sem=far_ssem.at[0], recv_sem=far_rsem.at[0],
            device_id={"py": dest // n_px, "px": lax.rem(dest, n_px)}, device_id_type=MESH,
        )

    def mirror_copy(u):
        return pltpu.make_async_remote_copy(
            src_ref=traces.at[:, rows_of(u), :], dst_ref=spans[u].at[mine],
            send_sem=m_ssem.at[u], recv_sem=m_rsem.at[u], device_id={"px": mirror}, device_id_type=MESH,
        )

    def held(u):
        return spans[u].at[mine] if units[u][0] == "M" else traces.at[:, rows_of(u), :]

    def gather_copy(u, k):
        return pltpu.make_async_remote_copy(
            src_ref=held(u), dst_ref=spans[u].at[mine], send_sem=g_ssem.at[u, k], recv_sem=g_rsem.at[u, k],
            device_id={"py": lax.rem(py + k, n_py)}, device_id_type=MESH,
        )

    def forwarded(u):
        return n_py == 4 and u >= DIRECT

    def near_copy(u, way):
        return pltpu.make_async_remote_copy(
            src_ref=held(u), dst_ref=spans[u].at[mine], send_sem=g_ssem.at[u, way], recv_sem=g_rsem.at[u, way],
            device_id={"py": across[way]}, device_id_type=MESH,
        )

    def far_half(u, way):
        part = spans[u].at[pl.ds(across[way] * loc + way * (loc // 2), loc // 2)]
        return pltpu.make_async_remote_copy(
            src_ref=part, dst_ref=part, send_sem=g_ssem.at[u, 2 + way], recv_sem=g_rsem.at[u, 2 + way],
            device_id={"py": across[1 - way]}, device_id_type=MESH,
        )

    def gather_start(u):
        if units[u][0] == "M":
            mirror_copy(u).wait_recv()
        if forwarded(u):
            for way in range(2):
                near_copy(u, way).start()
        else:
            run(1, n_py, lambda k: gather_copy(u, k).start())

    def gather_turn(u):
        if forwarded(u):
            for way in range(2):
                near_copy(u, way).wait_recv()
                far_half(u, way).start()

    def gather_end(u):
        if forwarded(u):
            for way in range(2):
                far_half(u, way).wait_recv()
        else:
            run(1, n_py, lambda k: gather_copy(u, k).wait_recv())
        if units[u][0] != "M":
            owns[u].wait()

    def gather_sent(u):
        if forwarded(u):
            for way in range(2):
                near_copy(u, way).wait_send()
                far_half(u, way).wait_send()
        else:
            run(1, n_py, lambda k: gather_copy(u, k).wait_send())

    def reach(u):
        return n_px if units[u][0] == "D" else side

    def x_dest(u, k):
        return lax.rem(px + k, n_px) if units[u][0] == "D" else base + lax.rem(px - base + k, side)

    def staged(u, dest):
        return n_px - 1 - dest if units[u][0] == "M" else dest

    def frames_at(u):
        source = mirror if units[u][0] == "M" else px
        return pl.ds(pl.multiple_of(source * wid, wid), wid)

    def x_copy(c, k):
        u, low, many = pieces[c]
        rows = rows_of(u)
        group = pl.ds(low, many)
        dest = x_dest(u, k)
        target = recv.at[group, rows, frames_at(u)] if direct else land.at[px, group, rows, :]
        return pltpu.make_async_remote_copy(
            src_ref=outb.at[staged(u, dest), group, rows, :],
            dst_ref=target,
            send_sem=x_ssem.at[c, k], recv_sem=x_rsem.at[c, k],
            device_id={"px": dest}, device_id_type=MESH,
        )

    for k in range(1, n_px):
        id_copy(k).start()
    for u in range(AHEAD):
        if u == AHEAD - 1:
            for v, unit in enumerate(units):
                if unit[0] == "M":
                    mirror_copy(v).start()
        gather_start(u)
    get_movie.start()
    get_foot.start()
    run(1, n_px, lambda k: id_copy(k).wait())
    to_smem = pltpu.make_async_copy(id_all, id_smem, local_sem.at[3])
    to_smem.start()
    to_smem.wait()

    def pick(dest, s, u):
        number = id_smem[dest, 0, s]
        ok = ((number >= 0) & (number < nblk)).astype(F32).astype(BF)
        index = jnp.minimum(jnp.maximum(number, 0), nblk - 1)
        return spans[u][index] * ok

    def deal(c):
        u, low, many = pieces[c]
        rows = rows_of(u)

        def route(k):
            dest = x_dest(u, k)
            for s in range(low, low + many):
                outb[staged(u, dest), s, rows, :] = pick(dest, s, u)
            x_copy(c, k).start()

        run(1, reach(u), route)
        for s in range(low, low + many):
            if direct:
                recv[s, rows, frames_at(u)] = pick(px, s, u)
            else:
                land[px, s, rows, :] = pick(px, s, u)

    for u in range(len(units) + 1):
        if u < len(units):
            gather_turn(u)
            if u + AHEAD < len(units):
                gather_start(u + AHEAD)
        if u:
            gather_end(u - 1)
            if u == 1:
                run(1, total, lambda k: far_copy(k).start())
            deal(u - 1)
    for c in range(len(units), len(pieces)):
        deal(c)

    pltpu.make_async_copy(far_ids, far_ids, far_rsem.at[0]).wait()
    to_far = pltpu.make_async_copy(far_ids, far_smem, local_sem.at[7])
    to_far.start()
    get_foot.wait()
    get_movie.wait()
    live = live_row[...]
    part = min(pixels, 512)
    frames = recv.shape[2]

    def cross_part(low, i):
        at = pl.ds(pl.multiple_of(i * part, part), part)
        cols = pl.ds(low * blk, pair * blk)
        crs[at, cols] = lax.dot_general(
            y_buf[at, :], recv[low : low + pair].reshape(pair * blk, frames), (((1,), (1,)), ((), ())),
            preferred_element_type=F32,
        )

    def age(i):
        at = pl.ds(pl.multiple_of(i * part, part), part)
        cur[at, :] = cur[at, :] * live

    run(0, pixels // part, age)
    to_far.wait()

    def spread(k):
        mat = jnp.zeros((slots, blk), jnp.int32)
        for s in range(slots):
            mat = jnp.where(sub == s, far_smem[k, 0, s], mat)
        far_mat[k] = mat

    run(0, total - 1, spread)
    for c, (u, low, many) in enumerate(pieces):
        for k in range(1, reach(u)):
            x_copy(c, k).wait_recv()
        if many == slots > 1 or u < len(units) - 1:
            continue
        if not direct:
            pack = 128 // wid
            for q in range(n_px // pack):
                both = [land[q * pack + j, low : low + many] for j in range(pack)]
                recv[low : low + many, :, q * 128 : (q + 1) * 128] = jnp.concatenate(both, axis=-1)
        run(0, pixels // part, lambda i: cross_part(low, i))
        near = slice(low * blk, (low + many) * blk)
        far = slice(0, (low + many) * blk)
        fresh_rows = lax.dot_general(
            recv[low : low + many].reshape(many * blk, frames), recv[: low + many].reshape((low + many) * blk, frames),
            (((1,), (1,)), ((), ())), preferred_element_type=F32,
        )
        gram_buf[near, far] = fresh_rows
        if low:
            gram_buf[: low * blk, near] = fresh_rows[:, : low * blk].T

    gram = gram_buf[...]
    eye = lax.broadcasted_iota(jnp.int32, (width, width), 0) == lax.broadcasted_iota(jnp.int32, (width, width), 1)
    denom = jnp.sum(jnp.where(eye, gram, 0.0), axis=0, keepdims=True) + 1e-06 + (1.0 - live)
    inv = 1.0 / denom
    hi, lo = split(jnp.where(eye, 1.0, 0.0) - gram * inv)
    for s in range(slots):
        hilo[s, :, :blk] = hi[:, s * blk : (s + 1) * blk]
        hilo[s, :, blk:] = lo[:, s * blk : (s + 1) * blk]
    def total_copy(step, k):
        dest = lax.rem(me + k, total)
        return pltpu.make_async_remote_copy(
            src_ref=t_send.at[step], dst_ref=t_recv.at[step, k - 1],
            send_sem=t_ssem.at[step], recv_sem=t_rsem.at[step],
            device_id={"py": dest // n_px, "px": lax.rem(dest, n_px)}, device_id_type=MESH,
        )

    def total_start(step):
        if n_py != 4:
            run(1, total, lambda k: total_copy(step, k).start())
            return
        upper = px // side
        for row in (n_py - 1 - py, across[0], across[1], py):

            def one(j):
                dest = row * n_px + (1 - upper) * (n_px - 1 - j) + upper * j
                k = lax.rem(dest - me + total, total)
                if row is py:
                    pl.when(k > 0)(lambda: total_copy(step, k).start())
                else:
                    total_copy(step, k).start()

            for j in range(n_px):
                one(j)

    scale = jnp.ones((1, width), F32)
    for step in range(ITERS):

        def sweep(i, sums, scale=scale):
            ats = [pl.ds(pl.multiple_of(i * whole + h * half_rows, half_rows), half_rows) for h in range(HALVES)]
            his, los = [], []
            for at in ats:
                now = cur[at, :] if step == 0 else cur[at, :] * scale
                both = [split(now[:, s * blk : (s + 1) * blk]) for s in range(slots)]
                his.append([b[0] for b in both])
                los.append([b[1] for b in both])
            squares = []
            for s in range(slots):
                m = hilo[s]
                low = slice(s * blk, (s + 1) * blk)
                prods = []
                for h in range(HALVES):
                    wide = mm(jnp.concatenate(his[h], axis=1), m)
                    thin = mm(jnp.concatenate(los[h], axis=1), m[:, :blk])
                    prods.append(wide[:, :blk] + wide[:, blk:] + thin)
                square = jnp.zeros((1, blk), F32)
                for h, at in enumerate(ats):
                    fresh = jnp.maximum(crs[at, low] * inv[:, low] + prods[h], 0.0)
                    cur[at, low] = fresh
                    his[h][s], los[h][s] = split(fresh)
                    square = square + jnp.sum(fresh * fresh, axis=0, keepdims=True)
                squares.append(square)
            return sums + jnp.concatenate(squares, axis=1)

        whole = min(pixels, 1024)
        half_rows = whole // HALVES
        sums = lax.fori_loop(0, pixels // whole, sweep, jnp.zeros((1, width), F32))
        for s in range(slots):
            t_send[step, s : s + 1, :] = sums[:, s * blk : (s + 1) * blk]
        total_start(step)
        if step == 0:
            for u, unit in enumerate(units):
                gather_sent(u)
                if unit[0] == "M":
                    mirror_copy(u).wait_send()
            for c, (u, low, many) in enumerate(pieces):
                run(1, reach(u), lambda k: x_copy(c, k).wait_send())
            pltpu.make_async_copy(far_ids, far_ids, far_ssem.at[0]).wait()
        pltpu.make_async_copy(t_recv.at[step], t_recv.at[step], t_rsem.at[step]).wait()
        got = t_recv[step]
        scales = []
        for s in range(slots):
            acc = sums[:, s * blk : (s + 1) * blk]
            same = jnp.where(far_mat[...] == ids[0, 0, s], got, 0.0)
            acc = acc + jnp.sum(jnp.sum(same, axis=0), axis=0, keepdims=True)
            scales.append(1.0 / jnp.sqrt(acc / (pixels * total) + 1e-06))
        scale = jnp.concatenate(scales, axis=1) * live
    scale_out[...] = scale

    for step in range(ITERS):
        pltpu.make_async_copy(t_recv.at[step], t_recv.at[step], t_ssem.at[step]).wait()


def per_device(n_py, n_px, movie, traces, footprints, block_ids):
    rows, cols, frames = movie.shape
    pixels = rows * cols
    width = footprints.shape[-1]
    slots = block_ids.shape[-1]
    blk = width // slots
    wid = traces.shape[1]
    loc = traces.shape[0] // blk
    total = n_py * n_px
    units = units_of(n_py, n_px, wid)
    pieces = pieces_of(units, slots)
    hbm = pl.BlockSpec(memory_space=pltpu.VMEM)
    dma = pltpu.SemaphoreType.DMA
    current, scale = pl.pallas_call(
        functools.partial(kernel, n_py, n_px),
        out_shape=(
            jax.ShapeDtypeStruct((pixels, width), F32),
            jax.ShapeDtypeStruct((1, width), F32),
        ),
        in_specs=[pl.BlockSpec(memory_space=pltpu.HBM)] * 3 + [pl.BlockSpec(memory_space=pltpu.SMEM)],
        out_specs=(hbm, pl.BlockSpec(memory_space=pltpu.VMEM)),
        scratch_shapes=[
            pltpu.VMEM((pixels, frames), BF),
            pltpu.VMEM((n_px, slots, blk, wid), BF),
            pltpu.VMEM((slots, blk, frames), BF),
            pltpu.VMEM((8, 128) if wid % 128 == 0 else (n_px, slots, blk, wid), BF),
            pltpu.VMEM((pixels, width), F32),
            pltpu.VMEM((slots, width, 2 * blk), BF),
            pltpu.VMEM((1, 128), jnp.int32),
            pltpu.VMEM((n_px, 1, 128), jnp.int32),
            pltpu.SMEM((n_px, 1, 128), jnp.int32),
            pltpu.VMEM((ITERS, slots, blk), F32),
            pltpu.VMEM((ITERS, total - 1, slots, blk), F32),
            pltpu.VMEM((1, width), F32),
            pltpu.VMEM((width, width), F32),
            dma((8,)), dma((len(units),)),
            dma((n_px,)), dma((n_px,)),
            dma((len(units), n_py)), dma((len(units), n_py)),
            dma((len(pieces), n_px)), dma((len(pieces), n_px)),
            dma((ITERS,)), dma((ITERS,)),
            dma((len(units),)), dma((len(units),)),
            pltpu.VMEM((total - 1, 1, 128), jnp.int32),
            pltpu.SMEM((total - 1, 1, 128), jnp.int32),
            pltpu.VMEM((total - 1, slots, blk), jnp.int32),
            dma((1,)), dma((1,)),
            *[pltpu.VMEM((loc * n_py, unit[2] * (blk // CHUNKS), wid), BF) for unit in units],
        ],
        compiler_params=pltpu.CompilerParams(
            collective_id=0, has_side_effects=True, vmem_limit_bytes=28 * 2**20
        ),
    )(
        pltpu.with_memory_space_constraint(movie.reshape(pixels, frames), pltpu.HBM),
        pltpu.with_memory_space_constraint(traces.reshape(loc, blk, wid), pltpu.HBM),
        pltpu.with_memory_space_constraint(footprints.reshape(pixels, width), pltpu.HBM),
        pltpu.with_memory_space_constraint(block_ids, pltpu.HBM),
    )
    def finish(a, b, o, buf, sem):
        n = 4
        q = pixels // n
        cps = [pltpu.make_async_copy(buf.at[i], o.at[pl.ds(i * q, q)], sem.at[i]) for i in range(n)]
        for i in range(n):
            buf[i] = a[pl.ds(i * q, q), :] * b[...]
            cps[i].start()
        for c in cps:
            c.wait()

    vm = pl.BlockSpec(memory_space=pltpu.VMEM)
    done = pl.pallas_call(
        finish, out_shape=jax.ShapeDtypeStruct((pixels, width), F32), in_specs=[vm, vm],
        out_specs=pl.BlockSpec(memory_space=pltpu.HBM),
        scratch_shapes=[pltpu.VMEM((4, pixels // 4, width), F32), dma((4,))],
        compiler_params=pltpu.CompilerParams(vmem_limit_bytes=28 * 2**20),
    )(current, scale)
    return done.reshape(rows, cols, width)


def solution(mesh):
    return jax.shard_map(
        functools.partial(per_device, mesh.shape["py"], mesh.shape["px"]),
        mesh=mesh,
        in_specs=(P("py", "px", None), P("py", "px"), P("py", "px", None), P("py", "px", None)),
        out_specs=P("py", "px", None),
        check_vma=False,
    )
```

```python
import functools

import jax
import jax.numpy as jnp
from jax import lax
from jax.experimental import pallas as pl
from jax.experimental.pallas import tpu as pltpu
from jax.sharding import PartitionSpec as P

ITERS = 2
CHUNKS = 8
AHEAD = 2
LATE = 4
HALVES = 2
DIRECT = 0
PLAN = (("D", 0, 1), ("O", 4, 1), ("D", 1, 1), ("D", 2, 1), ("D", 3, 1), ("M", 4, 1), ("O", 5, 1), ("M", 5, 1), ("O", 6, 1), ("M", 6, 1), ("O", 7, 1), ("M", 7, 1))
MESH = pl.DeviceIdType.MESH
BF = jnp.bfloat16
F32 = jnp.float32


def split(x):
    hi = x.astype(BF)
    return hi, (x - hi.astype(F32)).astype(BF)


def mm(a, b):
    return lax.dot_general(a, b, (((1,), (0,)), ((), ())), preferred_element_type=F32)


def units_of(n_py, n_px, wid):
    if wid % 128 == 0 and n_px % 4 == 0 and n_py == 4:
        return PLAN
    return tuple(("D", c, 1) for c in range(CHUNKS))


def pieces_of(units, slots):
    pair = max(slots // 2, 1)
    early = len(units) - LATE
    pieces = [(u, 0, slots) for u in range(early)]
    return pieces + [(u, s, pair) for s in range(0, slots, pair) for u in range(early, len(units))]


def kernel(
    n_py, n_px, movie, traces, foot, ids, cur_out, scale_out,
    y_buf, outb, recv, land, crs, hilo, id_row, id_all, id_smem, t_send, t_recv, live_row, gram_buf,
    local_sem, own_sem, id_ssem, id_rsem, g_ssem, g_rsem, x_ssem, x_rsem, t_ssem, t_rsem, m_ssem, m_rsem,
    far_ids, far_smem, far_mat, far_ssem, far_rsem, twin, *spans,
):
    py, px = lax.axis_index("py"), lax.axis_index("px")
    cur = cur_out
    total = n_py * n_px
    me = py * n_px + px
    loc, blk, wid = traces.shape
    nblk = loc * n_py
    slots = recv.shape[0]
    width = slots * blk
    direct = wid % 128 == 0
    pixels = y_buf.shape[0]
    step_rows = blk // CHUNKS
    units = units_of(n_py, n_px, wid)
    pieces = pieces_of(units, slots)
    pair = max(slots // 2, 1)
    nz = n_px // 2
    mirror = (nz - 1 - px // 2) * 2 + lax.rem(px, 2)
    side = n_px // 2
    base = (px // side) * side
    mine = pl.ds(py * loc, loc)
    across = [(py // 2) * 2 + 1 - lax.rem(py, 2), (1 - py // 2) * 2 + lax.rem(py, 2)]

    def rows_of(u):
        return pl.ds(units[u][1] * step_rows, units[u][2] * step_rows)

    barrier = pltpu.get_barrier_semaphore()

    def greet(device):
        pl.semaphore_signal(barrier, inc=1, device_id=device, device_id_type=MESH)

    def run(lo, hi, fn):
        def body(k, carry):
            fn(k)
            return carry

        lax.fori_loop(lo, hi, body, 0)

    for k in range(1, n_px):
        greet({"px": lax.rem(px + k, n_px)})
    for k in range(1, n_py):
        greet({"py": lax.rem(py + k, n_py)})

    owns = {
        u: pltpu.make_async_copy(traces.at[:, rows_of(u), :], spans[u].at[mine], own_sem.at[u])
        for u, unit in enumerate(units)
        if unit[0] != "M"
    }
    for own in owns.values():
        own.start()
    get_foot = pltpu.make_async_copy(foot, cur, local_sem.at[1])
    get_movie = pltpu.make_async_copy(movie, y_buf, local_sem.at[2])

    lane = lax.broadcasted_iota(jnp.int32, (1, 128), 1)
    row = jnp.zeros((1, 128), jnp.int32)
    for s in range(slots):
        row = jnp.where(lane == s, ids[0, 0, s], row)
    id_row[...] = row
    id_all[px] = row

    fill = jnp.zeros((slots, blk), jnp.int32)
    sub = lax.broadcasted_iota(jnp.int32, (slots, blk), 0)
    for s in range(slots):
        fill = jnp.where(sub == s, ids[0, 0, s], fill)
    for s in range(slots):
        alive = ((fill[s : s + 1, :] >= 0) & (fill[s : s + 1, :] < nblk)).astype(F32)
        live_row[:, s * blk : (s + 1) * blk] = alive
    pl.semaphore_wait(barrier, n_px - 1 + n_py - 1)

    def id_copy(k):
        return pltpu.make_async_remote_copy(
            src_ref=id_row, dst_ref=id_all.at[px], send_sem=id_ssem.at[k], recv_sem=id_rsem.at[k],
            device_id={"px": lax.rem(px + k, n_px)}, device_id_type=MESH,
        )

    def far_copy(k):
        dest = lax.rem(me + k, total)
        return pltpu.make_async_remote_copy(
            src_ref=id_row, dst_ref=far_ids.at[k - 1], send_sem=far_ssem.at[0], recv_sem=far_rsem.at[0],
            device_id={"py": dest // n_px, "px": lax.rem(dest, n_px)}, device_id_type=MESH,
        )

    def mirror_copy(u):
        return pltpu.make_async_remote_copy(
            src_ref=traces.at[:, rows_of(u), :], dst_ref=spans[u].at[mine],
            send_sem=m_ssem.at[u], recv_sem=m_rsem.at[u], device_id={"px": mirror}, device_id_type=MESH,
        )

    def held(u):
        return spans[u].at[mine] if units[u][0] == "M" else traces.at[:, rows_of(u), :]

    def gather_copy(u, k):
        return pltpu.make_async_remote_copy(
            src_ref=held(u), dst_ref=spans[u].at[mine], send_sem=g_ssem.at[u, k], recv_sem=g_rsem.at[u, k],
            device_id={"py": lax.rem(py + k, n_py)}, device_id_type=MESH,
        )

    def forwarded(u):
        return n_py == 4 and u >= DIRECT

    def near_copy(u, way):
        return pltpu.make_async_remote_copy(
            src_ref=held(u), dst_ref=spans[u].at[mine], send_sem=g_ssem.at[u, way], recv_sem=g_rsem.at[u, way],
            device_id={"py": across[way]}, device_id_type=MESH,
        )

    def far_half(u, way):
        part = spans[u].at[pl.ds(across[way] * loc + way * (loc // 2), loc // 2)]
        return pltpu.make_async_remote_copy(
            src_ref=part, dst_ref=part, send_sem=g_ssem.at[u, 2 + way], recv_sem=g_rsem.at[u, 2 + way],
            device_id={"py": across[1 - way]}, device_id_type=MESH,
        )

    def gather_start(u):
        if units[u][0] == "M":
            mirror_copy(u).wait_recv()
        if forwarded(u):
            for way in range(2):
                near_copy(u, way).start()
        else:
            run(1, n_py, lambda k: gather_copy(u, k).start())

    def gather_turn(u):
        if forwarded(u):
            for way in range(2):
                near_copy(u, way).wait_recv()
                far_half(u, way).start()

    def gather_end(u):
        if forwarded(u):
            for way in range(2):
                far_half(u, way).wait_recv()
        else:
            run(1, n_py, lambda k: gather_copy(u, k).wait_recv())
        if units[u][0] != "M":
            owns[u].wait()

    def gather_sent(u):
        if forwarded(u):
            for way in range(2):
                near_copy(u, way).wait_send()
                far_half(u, way).wait_send()
        else:
            run(1, n_py, lambda k: gather_copy(u, k).wait_send())

    def reach(u):
        return n_px if units[u][0] == "D" else side

    def x_dest(u, k):
        return lax.rem(px + k, n_px) if units[u][0] == "D" else base + lax.rem(px - base + k, side)

    def staged(u, dest):
        return n_px - 1 - dest if units[u][0] == "M" else dest

    def frames_at(u):
        source = mirror if units[u][0] == "M" else px
        return pl.ds(pl.multiple_of(source * wid, wid), wid)

    def x_copy(c, k):
        u, low, many = pieces[c]
        rows = rows_of(u)
        group = pl.ds(low, many)
        dest = x_dest(u, k)
        target = recv.at[group, rows, frames_at(u)] if direct else land.at[px, group, rows, :]
        return pltpu.make_async_remote_copy(
            src_ref=outb.at[staged(u, dest), group, rows, :],
            dst_ref=target,
            send_sem=x_ssem.at[c, k], recv_sem=x_rsem.at[c, k],
            device_id={"px": dest}, device_id_type=MESH,
        )

    for k in range(1, n_px):
        id_copy(k).start()
    for u in range(AHEAD):
        if u == AHEAD - 1:
            for v, unit in enumerate(units):
                if unit[0] == "M":
                    mirror_copy(v).start()
        gather_start(u)
    get_movie.start()
    get_foot.start()
    run(1, n_px, lambda k: id_copy(k).wait())
    to_smem = pltpu.make_async_copy(id_all, id_smem, local_sem.at[3])
    to_smem.start()
    to_smem.wait()

    def pick(dest, s, u):
        number = id_smem[dest, 0, s]
        ok = ((number >= 0) & (number < nblk)).astype(F32).astype(BF)
        index = jnp.minimum(jnp.maximum(number, 0), nblk - 1)
        return spans[u][index] * ok

    def deal(c):
        u, low, many = pieces[c]
        rows = rows_of(u)

        def route(k):
            dest = x_dest(u, k)
            for s in range(low, low + many):
                outb[staged(u, dest), s, rows, :] = pick(dest, s, u)
            x_copy(c, k).start()

        run(1, reach(u), route)
        for s in range(low, low + many):
            if direct:
                recv[s, rows, frames_at(u)] = pick(px, s, u)
            else:
                land[px, s, rows, :] = pick(px, s, u)

    for u in range(len(units) + 1):
        if u < len(units):
            gather_turn(u)
            if u + AHEAD < len(units):
                gather_start(u + AHEAD)
        if u:
            gather_end(u - 1)
            if u == 1:
                run(1, total, lambda k: far_copy(k).start())
            deal(u - 1)
    for c in range(len(units), len(pieces)):
        deal(c)

    pltpu.make_async_copy(far_ids, far_ids, far_rsem.at[0]).wait()
    to_far = pltpu.make_async_copy(far_ids, far_smem, local_sem.at[7])
    to_far.start()
    get_foot.wait()
    get_movie.wait()
    live = live_row[...]
    part = min(pixels, 512)
    frames = recv.shape[2]

    def cross_part(low, i):
        at = pl.ds(pl.multiple_of(i * part, part), part)
        cols = pl.ds(low * blk, pair * blk)
        crs[at, cols] = lax.dot_general(
            y_buf[at, :], recv[low : low + pair].reshape(pair * blk, frames), (((1,), (1,)), ((), ())),
            preferred_element_type=F32,
        )

    def age(i):
        at = pl.ds(pl.multiple_of(i * part, part), part)
        cur[at, :] = cur[at, :] * live

    run(0, pixels // part, age)
    to_far.wait()

    def spread(k):
        mat = jnp.zeros((slots, blk), jnp.int32)
        for s in range(slots):
            mat = jnp.where(sub == s, far_smem[k, 0, s], mat)
        far_mat[k] = mat

    run(0, total - 1, spread)
    for c, (u, low, many) in enumerate(pieces):
        for k in range(1, reach(u)):
            x_copy(c, k).wait_recv()
        if many == slots > 1 or u < len(units) - 1:
            continue
        if not direct:
            pack = 128 // wid
            for q in range(n_px // pack):
                both = [land[q * pack + j, low : low + many] for j in range(pack)]
                recv[low : low + many, :, q * 128 : (q + 1) * 128] = jnp.concatenate(both, axis=-1)
        run(0, pixels // part, lambda i: cross_part(low, i))
        near = slice(low * blk, (low + many) * blk)
        far = slice(0, (low + many) * blk)
        fresh_rows = lax.dot_general(
            recv[low : low + many].reshape(many * blk, frames), recv[: low + many].reshape((low + many) * blk, frames),
            (((1,), (1,)), ((), ())), preferred_element_type=F32,
        )
        gram_buf[near, far] = fresh_rows
        if low:
            gram_buf[: low * blk, near] = fresh_rows[:, : low * blk].T

    gram = gram_buf[...]
    eye = lax.broadcasted_iota(jnp.int32, (width, width), 0) == lax.broadcasted_iota(jnp.int32, (width, width), 1)
    denom = jnp.sum(jnp.where(eye, gram, 0.0), axis=0, keepdims=True) + 1e-06 + (1.0 - live)
    inv = 1.0 / denom
    hi, lo = split(jnp.where(eye, 1.0, 0.0) - gram * inv)
    for s in range(slots):
        hilo[s, :, :blk] = hi[:, s * blk : (s + 1) * blk]
        hilo[s, :, blk:] = lo[:, s * blk : (s + 1) * blk]
    for p in range(slots // 2):
        twin[p] = hi[:, 2 * p * blk : 2 * (p + 1) * blk]
        twin[p, 2 * p * blk : (2 * p + 1) * blk, blk:] = jnp.zeros((blk, blk), BF)
    def total_copy(step, k):
        dest = lax.rem(me + k, total)
        return pltpu.make_async_remote_copy(
            src_ref=t_send.at[step], dst_ref=t_recv.at[step, k - 1],
            send_sem=t_ssem.at[step], recv_sem=t_rsem.at[step],
            device_id={"py": dest // n_px, "px": lax.rem(dest, n_px)}, device_id_type=MESH,
        )

    def total_start(step):
        if n_py != 4:
            run(1, total, lambda k: total_copy(step, k).start())
            return
        upper = px // side
        for row in (n_py - 1 - py, across[0], across[1], py):

            def one(j):
                dest = row * n_px + (1 - upper) * (n_px - 1 - j) + upper * j
                k = lax.rem(dest - me + total, total)
                if row is py:
                    pl.when(k > 0)(lambda: total_copy(step, k).start())
                else:
                    total_copy(step, k).start()

            for j in range(n_px):
                one(j)

    scale = jnp.ones((1, width), F32)
    for step in range(ITERS):

        def sweep(i, sums, scale=scale):
            ats = [pl.ds(pl.multiple_of(i * whole + h * half_rows, half_rows), half_rows) for h in range(HALVES)]
            his, los = [], []
            for at in ats:
                now = cur[at, :] if step == 0 else cur[at, :] * scale
                both = [split(now[:, s * blk : (s + 1) * blk]) for s in range(slots)]
                his.append([b[0] for b in both])
                los.append([b[1] for b in both])
            squares, pairs = [], {}
            for s in range(slots):
                m = hilo[s]
                low = slice(s * blk, (s + 1) * blk)
                prods = []
                for h in range(HALVES):
                    wide = mm(jnp.concatenate(his[h], axis=1), m)
                    if s % 2 == 0 and s + 1 < slots:
                        pairs[h] = mm(jnp.concatenate(los[h], axis=1), twin[s // 2])
                        thin = pairs[h][:, :blk]
                    elif s % 2:
                        thin = pairs[h][:, blk:] + mm(los[h][s - 1], m[(s - 1) * blk : s * blk, :blk])
                    else:
                        thin = mm(jnp.concatenate(los[h], axis=1), m[:, :blk])
                    prods.append(wide[:, :blk] + wide[:, blk:] + thin)
                square = jnp.zeros((1, blk), F32)
                for h, at in enumerate(ats):
                    fresh = jnp.maximum(crs[at, low] * inv[:, low] + prods[h], 0.0)
                    cur[at, low] = fresh
                    his[h][s], los[h][s] = split(fresh)
                    square = square + jnp.sum(fresh * fresh, axis=0, keepdims=True)
                squares.append(square)
            return sums + jnp.concatenate(squares, axis=1)

        whole = min(pixels, 1024)
        half_rows = whole // HALVES
        sums = lax.fori_loop(0, pixels // whole, sweep, jnp.zeros((1, width), F32))
        for s in range(slots):
            t_send[step, s : s + 1, :] = sums[:, s * blk : (s + 1) * blk]
        total_start(step)
        if step == 0:
            for u, unit in enumerate(units):
                gather_sent(u)
                if unit[0] == "M":
                    mirror_copy(u).wait_send()
            for c, (u, low, many) in enumerate(pieces):
                run(1, reach(u), lambda k: x_copy(c, k).wait_send())
            pltpu.make_async_copy(far_ids, far_ids, far_ssem.at[0]).wait()
        pltpu.make_async_copy(t_recv.at[step], t_recv.at[step], t_rsem.at[step]).wait()
        got = t_recv[step]
        scales = []
        for s in range(slots):
            acc = sums[:, s * blk : (s + 1) * blk]
            same = jnp.where(far_mat[...] == ids[0, 0, s], got, 0.0)
            acc = acc + jnp.sum(jnp.sum(same, axis=0), axis=0, keepdims=True)
            scales.append(1.0 / jnp.sqrt(acc / (pixels * total) + 1e-06))
        scale = jnp.concatenate(scales, axis=1) * live
    scale_out[...] = scale

    for step in range(ITERS):
        pltpu.make_async_copy(t_recv.at[step], t_recv.at[step], t_ssem.at[step]).wait()


def per_device(n_py, n_px, movie, traces, footprints, block_ids):
    rows, cols, frames = movie.shape
    pixels = rows * cols
    width = footprints.shape[-1]
    slots = block_ids.shape[-1]
    blk = width // slots
    wid = traces.shape[1]
    loc = traces.shape[0] // blk
    total = n_py * n_px
    units = units_of(n_py, n_px, wid)
    pieces = pieces_of(units, slots)
    hbm = pl.BlockSpec(memory_space=pltpu.VMEM)
    dma = pltpu.SemaphoreType.DMA
    current, scale = pl.pallas_call(
        functools.partial(kernel, n_py, n_px),
        out_shape=(
            jax.ShapeDtypeStruct((pixels, width), F32),
            jax.ShapeDtypeStruct((1, width), F32),
        ),
        in_specs=[pl.BlockSpec(memory_space=pltpu.HBM)] * 3 + [pl.BlockSpec(memory_space=pltpu.SMEM)],
        out_specs=(hbm, pl.BlockSpec(memory_space=pltpu.VMEM)),
        scratch_shapes=[
            pltpu.VMEM((pixels, frames), BF),
            pltpu.VMEM((n_px, slots, blk, wid), BF),
            pltpu.VMEM((slots, blk, frames), BF),
            pltpu.VMEM((8, 128) if wid % 128 == 0 else (n_px, slots, blk, wid), BF),
            pltpu.VMEM((pixels, width), F32),
            pltpu.VMEM((slots, width, 2 * blk), BF),
            pltpu.VMEM((1, 128), jnp.int32),
            pltpu.VMEM((n_px, 1, 128), jnp.int32),
            pltpu.SMEM((n_px, 1, 128), jnp.int32),
            pltpu.VMEM((ITERS, slots, blk), F32),
            pltpu.VMEM((ITERS, total - 1, slots, blk), F32),
            pltpu.VMEM((1, width), F32),
            pltpu.VMEM((width, width), F32),
            dma((8,)), dma((len(units),)),
            dma((n_px,)), dma((n_px,)),
            dma((len(units), n_py)), dma((len(units), n_py)),
            dma((len(pieces), n_px)), dma((len(pieces), n_px)),
            dma((ITERS,)), dma((ITERS,)),
            dma((len(units),)), dma((len(units),)),
            pltpu.VMEM((total - 1, 1, 128), jnp.int32),
            pltpu.SMEM((total - 1, 1, 128), jnp.int32),
            pltpu.VMEM((total - 1, slots, blk), jnp.int32),
            dma((1,)), dma((1,)),
            pltpu.VMEM((max(slots // 2, 1), width, 2 * blk), BF),
            *[pltpu.VMEM((loc * n_py, unit[2] * (blk // CHUNKS), wid), BF) for unit in units],
        ],
        compiler_params=pltpu.CompilerParams(
            collective_id=0, has_side_effects=True, vmem_limit_bytes=28 * 2**20
        ),
    )(
        pltpu.with_memory_space_constraint(movie.reshape(pixels, frames), pltpu.HBM),
        pltpu.with_memory_space_constraint(traces.reshape(loc, blk, wid), pltpu.HBM),
        pltpu.with_memory_space_constraint(footprints.reshape(pixels, width), pltpu.HBM),
        pltpu.with_memory_space_constraint(block_ids, pltpu.HBM),
    )
    def finish(a, b, o, buf, sem):
        n = 4
        q = pixels // n
        cps = [pltpu.make_async_copy(buf.at[i], o.at[pl.ds(i * q, q)], sem.at[i]) for i in range(n)]
        for i in range(n):
            buf[i] = a[pl.ds(i * q, q), :] * b[...]
            cps[i].start()
        for c in cps:
            c.wait()

    vm = pl.BlockSpec(memory_space=pltpu.VMEM)
    done = pl.pallas_call(
        finish, out_shape=jax.ShapeDtypeStruct((pixels, width), F32), in_specs=[vm, vm],
        out_specs=pl.BlockSpec(memory_space=pltpu.HBM),
        scratch_shapes=[pltpu.VMEM((4, pixels // 4, width), F32), dma((4,))],
        compiler_params=pltpu.CompilerParams(vmem_limit_bytes=28 * 2**20),
    )(current, scale)
    return done.reshape(rows, cols, width)


def solution(mesh):
    return jax.shard_map(
        functools.partial(per_device, mesh.shape["py"], mesh.shape["px"]),
        mesh=mesh,
        in_specs=(P("py", "px", None), P("py", "px"), P("py", "px", None), P("py", "px", None)),
        out_specs=P("py", "px", None),
        check_vma=False,
    )
```

```python
import functools

import jax
import jax.numpy as jnp
from jax import lax
from jax.experimental import pallas as pl
from jax.experimental.pallas import tpu as pltpu
from jax.sharding import PartitionSpec as P

ITERS = 2
CHUNKS = 8
AHEAD = 2
LATE = 4
HALVES = 2
DIRECT = 0
PLAN = (("D", 0, 1), ("O", 4, 1), ("D", 1, 1), ("D", 2, 1), ("D", 3, 1), ("M", 4, 1), ("O", 5, 1), ("M", 5, 1), ("O", 6, 1), ("M", 6, 1), ("O", 7, 1), ("M", 7, 1))
MESH = pl.DeviceIdType.MESH
BF = jnp.bfloat16
F32 = jnp.float32


def split(x):
    hi = x.astype(BF)
    return hi, (x - hi.astype(F32)).astype(BF)


def mm(a, b):
    return lax.dot_general(a, b, (((1,), (0,)), ((), ())), preferred_element_type=F32)


def units_of(n_py, n_px, wid):
    if wid % 128 == 0 and n_px % 4 == 0 and n_py == 4:
        return PLAN
    return tuple(("D", c, 1) for c in range(CHUNKS))


def pieces_of(units, slots):
    pair = max(slots // 2, 1)
    early = len(units) - LATE
    pieces = [(u, 0, slots) for u in range(early)]
    return pieces + [(u, s, pair) for s in range(0, slots, pair) for u in range(early, len(units))]


def kernel(
    n_py, n_px, movie, traces, foot, ids, cur_out, scale_out,
    y_buf, outb, recv, land, crs, hilo, id_row, id_all, id_smem, t_send, t_recv, live_row, gram_buf,
    local_sem, own_sem, id_ssem, id_rsem, g_ssem, g_rsem, x_ssem, x_rsem, t_ssem, t_rsem, m_ssem, m_rsem,
    far_ids, far_smem, far_mat, far_ssem, far_rsem, twin, *spans,
):
    py, px = lax.axis_index("py"), lax.axis_index("px")
    cur = cur_out
    total = n_py * n_px
    me = py * n_px + px
    loc, blk, wid = traces.shape
    nblk = loc * n_py
    slots = recv.shape[0]
    width = slots * blk
    direct = wid % 128 == 0
    pixels = y_buf.shape[0]
    step_rows = blk // CHUNKS
    units = units_of(n_py, n_px, wid)
    pieces = pieces_of(units, slots)
    pair = max(slots // 2, 1)
    nz = n_px // 2
    mirror = (nz - 1 - px // 2) * 2 + lax.rem(px, 2)
    side = n_px // 2
    base = (px // side) * side
    mine = pl.ds(py * loc, loc)
    across = [(py // 2) * 2 + 1 - lax.rem(py, 2), (1 - py // 2) * 2 + lax.rem(py, 2)]

    def rows_of(u):
        return pl.ds(units[u][1] * step_rows, units[u][2] * step_rows)

    barrier = pltpu.get_barrier_semaphore()

    def greet(device):
        pl.semaphore_signal(barrier, inc=1, device_id=device, device_id_type=MESH)

    def run(lo, hi, fn):
        def body(k, carry):
            fn(k)
            return carry

        lax.fori_loop(lo, hi, body, 0)

    for k in range(1, n_px):
        greet({"px": lax.rem(px + k, n_px)})
    for k in range(1, n_py):
        greet({"py": lax.rem(py + k, n_py)})

    owns = {
        u: pltpu.make_async_copy(traces.at[:, rows_of(u), :], spans[u].at[mine], own_sem.at[u])
        for u, unit in enumerate(units)
        if unit[0] != "M"
    }
    for own in owns.values():
        own.start()
    get_foot = pltpu.make_async_copy(foot, cur, local_sem.at[1])
    get_movie = pltpu.make_async_copy(movie, y_buf, local_sem.at[2])

    lane = lax.broadcasted_iota(jnp.int32, (1, 128), 1)
    row = jnp.zeros((1, 128), jnp.int32)
    for s in range(slots):
        row = jnp.where(lane == s, ids[0, 0, s], row)
    id_row[...] = row
    id_all[px] = row

    fill = jnp.zeros((slots, blk), jnp.int32)
    sub = lax.broadcasted_iota(jnp.int32, (slots, blk), 0)
    for s in range(slots):
        fill = jnp.where(sub == s, ids[0, 0, s], fill)
    for s in range(slots):
        alive = ((fill[s : s + 1, :] >= 0) & (fill[s : s + 1, :] < nblk)).astype(F32)
        live_row[:, s * blk : (s + 1) * blk] = alive
    pl.semaphore_wait(barrier, n_px - 1 + n_py - 1)

    def id_copy(k):
        return pltpu.make_async_remote_copy(
            src_ref=id_row, dst_ref=id_all.at[px], send_sem=id_ssem.at[k], recv_sem=id_rsem.at[k],
            device_id={"px": lax.rem(px + k, n_px)}, device_id_type=MESH,
        )

    def far_copy(k):
        dest = lax.rem(me + k, total)
        return pltpu.make_async_remote_copy(
            src_ref=id_row, dst_ref=far_ids.at[k - 1], send_sem=far_ssem.at[0], recv_sem=far_rsem.at[0],
            device_id={"py": dest // n_px, "px": lax.rem(dest, n_px)}, device_id_type=MESH,
        )

    def mirror_copy(u):
        return pltpu.make_async_remote_copy(
            src_ref=traces.at[:, rows_of(u), :], dst_ref=spans[u].at[mine],
            send_sem=m_ssem.at[u], recv_sem=m_rsem.at[u], device_id={"px": mirror}, device_id_type=MESH,
        )

    def held(u):
        return spans[u].at[mine] if units[u][0] == "M" else traces.at[:, rows_of(u), :]

    def gather_copy(u, k):
        return pltpu.make_async_remote_copy(
            src_ref=held(u), dst_ref=spans[u].at[mine], send_sem=g_ssem.at[u, k], recv_sem=g_rsem.at[u, k],
            device_id={"py": lax.rem(py + k, n_py)}, device_id_type=MESH,
        )

    def forwarded(u):
        return n_py == 4 and u >= DIRECT

    def near_copy(u, way):
        return pltpu.make_async_remote_copy(
            src_ref=held(u), dst_ref=spans[u].at[mine], send_sem=g_ssem.at[u, way], recv_sem=g_rsem.at[u, way],
            device_id={"py": across[way]}, device_id_type=MESH,
        )

    def far_half(u, way):
        part = spans[u].at[pl.ds(across[way] * loc + way * (loc // 2), loc // 2)]
        return pltpu.make_async_remote_copy(
            src_ref=part, dst_ref=part, send_sem=g_ssem.at[u, 2 + way], recv_sem=g_rsem.at[u, 2 + way],
            device_id={"py": across[1 - way]}, device_id_type=MESH,
        )

    def gather_start(u):
        if units[u][0] == "M":
            mirror_copy(u).wait_recv()
        if forwarded(u):
            for way in range(2):
                near_copy(u, way).start()
        else:
            run(1, n_py, lambda k: gather_copy(u, k).start())

    def gather_turn(u):
        if forwarded(u):
            for way in range(2):
                near_copy(u, way).wait_recv()
                far_half(u, way).start()

    def gather_end(u):
        if forwarded(u):
            for way in range(2):
                far_half(u, way).wait_recv()
        else:
            run(1, n_py, lambda k: gather_copy(u, k).wait_recv())
        if units[u][0] != "M":
            owns[u].wait()

    def gather_sent(u):
        if forwarded(u):
            for way in range(2):
                near_copy(u, way).wait_send()
                far_half(u, way).wait_send()
        else:
            run(1, n_py, lambda k: gather_copy(u, k).wait_send())

    def reach(u):
        return n_px if units[u][0] == "D" else side

    def x_dest(u, k):
        return lax.rem(px + k, n_px) if units[u][0] == "D" else base + lax.rem(px - base + k, side)

    def staged(u, dest):
        return n_px - 1 - dest if units[u][0] == "M" else dest

    def frames_at(u):
        source = mirror if units[u][0] == "M" else px
        return pl.ds(pl.multiple_of(source * wid, wid), wid)

    def x_copy(c, k):
        u, low, many = pieces[c]
        rows = rows_of(u)
        group = pl.ds(low, many)
        dest = x_dest(u, k)
        target = recv.at[group, rows, frames_at(u)] if direct else land.at[px, group, rows, :]
        return pltpu.make_async_remote_copy(
            src_ref=outb.at[staged(u, dest), group, rows, :],
            dst_ref=target,
            send_sem=x_ssem.at[c, k], recv_sem=x_rsem.at[c, k],
            device_id={"px": dest}, device_id_type=MESH,
        )

    for k in range(1, n_px):
        id_copy(k).start()
    for u in range(AHEAD):
        if u == AHEAD - 1:
            for v, unit in enumerate(units):
                if unit[0] == "M":
                    mirror_copy(v).start()
        gather_start(u)
    get_movie.start()
    get_foot.start()
    run(1, n_px, lambda k: id_copy(k).wait())
    to_smem = pltpu.make_async_copy(id_all, id_smem, local_sem.at[3])
    to_smem.start()
    to_smem.wait()

    def pick(dest, s, u):
        number = id_smem[dest, 0, s]
        ok = ((number >= 0) & (number < nblk)).astype(F32).astype(BF)
        index = jnp.minimum(jnp.maximum(number, 0), nblk - 1)
        return spans[u][index] * ok

    def deal(c):
        u, low, many = pieces[c]
        rows = rows_of(u)

        def route(k):
            dest = x_dest(u, k)
            for s in range(low, low + many):
                outb[staged(u, dest), s, rows, :] = pick(dest, s, u)
            x_copy(c, k).start()

        run(1, reach(u), route)
        for s in range(low, low + many):
            if direct:
                recv[s, rows, frames_at(u)] = pick(px, s, u)
            else:
                land[px, s, rows, :] = pick(px, s, u)

    for u in range(len(units) + 1):
        if u < len(units):
            gather_turn(u)
            if u + AHEAD < len(units):
                gather_start(u + AHEAD)
        if u:
            gather_end(u - 1)
            if u == 1:
                run(1, total, lambda k: far_copy(k).start())
            deal(u - 1)
    for c in range(len(units), len(pieces)):
        deal(c)

    pltpu.make_async_copy(far_ids, far_ids, far_rsem.at[0]).wait()
    to_far = pltpu.make_async_copy(far_ids, far_smem, local_sem.at[7])
    to_far.start()
    get_foot.wait()
    get_movie.wait()
    live = live_row[...]
    part = min(pixels, 512)
    frames = recv.shape[2]

    def cross_part(low, i):
        at = pl.ds(pl.multiple_of(i * part, part), part)
        cols = pl.ds(low * blk, pair * blk)
        crs[at, cols] = lax.dot_general(
            y_buf[at, :], recv[low : low + pair].reshape(pair * blk, frames), (((1,), (1,)), ((), ())),
            preferred_element_type=F32,
        )

    def age(i):
        at = pl.ds(pl.multiple_of(i * part, part), part)
        cur[at, :] = cur[at, :] * live

    run(0, pixels // part, age)
    to_far.wait()

    def spread(k):
        mat = jnp.zeros((slots, blk), jnp.int32)
        for s in range(slots):
            mat = jnp.where(sub == s, far_smem[k, 0, s], mat)
        far_mat[k] = mat

    run(0, total - 1, spread)
    for c, (u, low, many) in enumerate(pieces):
        for k in range(1, reach(u)):
            x_copy(c, k).wait_recv()
        if many == slots > 1 or u < len(units) - 1:
            continue
        if not direct:
            pack = 128 // wid
            for q in range(n_px // pack):
                both = [land[q * pack + j, low : low + many] for j in range(pack)]
                recv[low : low + many, :, q * 128 : (q + 1) * 128] = jnp.concatenate(both, axis=-1)
        for i in range(pixels // part):
            cross_part(low, i)
        near = slice(low * blk, (low + many) * blk)
        far = slice(0, (low + many) * blk)
        fresh_rows = lax.dot_general(
            recv[low : low + many].reshape(many * blk, frames), recv[: low + many].reshape((low + many) * blk, frames),
            (((1,), (1,)), ((), ())), preferred_element_type=F32,
        )
        gram_buf[near, far] = fresh_rows
        if low:
            gram_buf[: low * blk, near] = fresh_rows[:, : low * blk].T

    gram = gram_buf[...]
    eye = lax.broadcasted_iota(jnp.int32, (width, width), 0) == lax.broadcasted_iota(jnp.int32, (width, width), 1)
    denom = jnp.sum(jnp.where(eye, gram, 0.0), axis=0, keepdims=True) + 1e-06 + (1.0 - live)
    inv = 1.0 / denom
    hi, lo = split(jnp.where(eye, 1.0, 0.0) - gram * inv)
    for s in range(slots):
        hilo[s, :, :blk] = hi[:, s * blk : (s + 1) * blk]
        hilo[s, :, blk:] = lo[:, s * blk : (s + 1) * blk]
    for p in range(slots // 2):
        twin[p] = hi[:, 2 * p * blk : 2 * (p + 1) * blk]
        twin[p, 2 * p * blk : (2 * p + 1) * blk, blk:] = jnp.zeros((blk, blk), BF)
    def total_copy(step, k):
        dest = lax.rem(me + k, total)
        return pltpu.make_async_remote_copy(
            src_ref=t_send.at[step], dst_ref=t_recv.at[step, k - 1],
            send_sem=t_ssem.at[step], recv_sem=t_rsem.at[step],
            device_id={"py": dest // n_px, "px": lax.rem(dest, n_px)}, device_id_type=MESH,
        )

    def total_start(step):
        if n_py != 4:
            run(1, total, lambda k: total_copy(step, k).start())
            return
        upper = px // side
        for row in (n_py - 1 - py, across[0], across[1], py):

            def one(j):
                dest = row * n_px + (1 - upper) * (n_px - 1 - j) + upper * j
                k = lax.rem(dest - me + total, total)
                if row is py:
                    pl.when(k > 0)(lambda: total_copy(step, k).start())
                else:
                    total_copy(step, k).start()

            for j in range(n_px):
                one(j)

    scale = jnp.ones((1, width), F32)
    for step in range(ITERS):

        def sweep(i, sums, scale=scale):
            ats = [pl.ds(pl.multiple_of(i * whole + h * half_rows, half_rows), half_rows) for h in range(HALVES)]
            his, los = [], []
            for at in ats:
                now = cur[at, :] if step == 0 else cur[at, :] * scale
                both = [split(now[:, s * blk : (s + 1) * blk]) for s in range(slots)]
                his.append([b[0] for b in both])
                los.append([b[1] for b in both])
            squares, pairs = [], {}
            for s in range(slots):
                m = hilo[s]
                low = slice(s * blk, (s + 1) * blk)
                prods = []
                for h in range(HALVES):
                    wide = mm(jnp.concatenate(his[h], axis=1), m)
                    if s % 2 == 0 and s + 1 < slots:
                        pairs[h] = mm(jnp.concatenate(los[h], axis=1), twin[s // 2])
                        thin = pairs[h][:, :blk]
                    elif s % 2:
                        thin = pairs[h][:, blk:] + mm(los[h][s - 1], m[(s - 1) * blk : s * blk, :blk])
                    else:
                        thin = mm(jnp.concatenate(los[h], axis=1), m[:, :blk])
                    prods.append(wide[:, :blk] + wide[:, blk:] + thin)
                square = jnp.zeros((1, blk), F32)
                for h, at in enumerate(ats):
                    fresh = jnp.maximum(crs[at, low] * inv[:, low] + prods[h], 0.0)
                    cur[at, low] = fresh
                    his[h][s], los[h][s] = split(fresh)
                    square = square + jnp.sum(fresh * fresh, axis=0, keepdims=True)
                squares.append(square)
            return sums + jnp.concatenate(squares, axis=1)

        whole = min(pixels, 1024)
        half_rows = whole // HALVES
        sums = lax.fori_loop(0, pixels // whole, sweep, jnp.zeros((1, width), F32))
        for s in range(slots):
            t_send[step, s : s + 1, :] = sums[:, s * blk : (s + 1) * blk]
        total_start(step)
        if step == 0:
            for u, unit in enumerate(units):
                gather_sent(u)
                if unit[0] == "M":
                    mirror_copy(u).wait_send()
            for c, (u, low, many) in enumerate(pieces):
                run(1, reach(u), lambda k: x_copy(c, k).wait_send())
            pltpu.make_async_copy(far_ids, far_ids, far_ssem.at[0]).wait()
        pltpu.make_async_copy(t_recv.at[step], t_recv.at[step], t_rsem.at[step]).wait()
        got = t_recv[step]
        scales = []
        for s in range(slots):
            acc = sums[:, s * blk : (s + 1) * blk]
            same = jnp.where(far_mat[...] == ids[0, 0, s], got, 0.0)
            acc = acc + jnp.sum(jnp.sum(same, axis=0), axis=0, keepdims=True)
            scales.append(1.0 / jnp.sqrt(acc / (pixels * total) + 1e-06))
        scale = jnp.concatenate(scales, axis=1) * live
    scale_out[...] = scale

    for step in range(ITERS):
        pltpu.make_async_copy(t_recv.at[step], t_recv.at[step], t_ssem.at[step]).wait()


def per_device(n_py, n_px, movie, traces, footprints, block_ids):
    rows, cols, frames = movie.shape
    pixels = rows * cols
    width = footprints.shape[-1]
    slots = block_ids.shape[-1]
    blk = width // slots
    wid = traces.shape[1]
    loc = traces.shape[0] // blk
    total = n_py * n_px
    units = units_of(n_py, n_px, wid)
    pieces = pieces_of(units, slots)
    hbm = pl.BlockSpec(memory_space=pltpu.VMEM)
    dma = pltpu.SemaphoreType.DMA
    current, scale = pl.pallas_call(
        functools.partial(kernel, n_py, n_px),
        out_shape=(
            jax.ShapeDtypeStruct((pixels, width), F32),
            jax.ShapeDtypeStruct((1, width), F32),
        ),
        in_specs=[pl.BlockSpec(memory_space=pltpu.HBM)] * 3 + [pl.BlockSpec(memory_space=pltpu.SMEM)],
        out_specs=(hbm, pl.BlockSpec(memory_space=pltpu.VMEM)),
        scratch_shapes=[
            pltpu.VMEM((pixels, frames), BF),
            pltpu.VMEM((n_px, slots, blk, wid), BF),
            pltpu.VMEM((slots, blk, frames), BF),
            pltpu.VMEM((8, 128) if wid % 128 == 0 else (n_px, slots, blk, wid), BF),
            pltpu.VMEM((pixels, width), F32),
            pltpu.VMEM((slots, width, 2 * blk), BF),
            pltpu.VMEM((1, 128), jnp.int32),
            pltpu.VMEM((n_px, 1, 128), jnp.int32),
            pltpu.SMEM((n_px, 1, 128), jnp.int32),
            pltpu.VMEM((ITERS, slots, blk), F32),
            pltpu.VMEM((ITERS, total - 1, slots, blk), F32),
            pltpu.VMEM((1, width), F32),
            pltpu.VMEM((width, width), F32),
            dma((8,)), dma((len(units),)),
            dma((n_px,)), dma((n_px,)),
            dma((len(units), n_py)), dma((len(units), n_py)),
            dma((len(pieces), n_px)), dma((len(pieces), n_px)),
            dma((ITERS,)), dma((ITERS,)),
            dma((len(units),)), dma((len(units),)),
            pltpu.VMEM((total - 1, 1, 128), jnp.int32),
            pltpu.SMEM((total - 1, 1, 128), jnp.int32),
            pltpu.VMEM((total - 1, slots, blk), jnp.int32),
            dma((1,)), dma((1,)),
            pltpu.VMEM((max(slots // 2, 1), width, 2 * blk), BF),
            *[pltpu.VMEM((loc * n_py, unit[2] * (blk // CHUNKS), wid), BF) for unit in units],
        ],
        compiler_params=pltpu.CompilerParams(
            collective_id=0, has_side_effects=True, vmem_limit_bytes=28 * 2**20
        ),
    )(
        pltpu.with_memory_space_constraint(movie.reshape(pixels, frames), pltpu.HBM),
        pltpu.with_memory_space_constraint(traces.reshape(loc, blk, wid), pltpu.HBM),
        pltpu.with_memory_space_constraint(footprints.reshape(pixels, width), pltpu.HBM),
        pltpu.with_memory_space_constraint(block_ids, pltpu.HBM),
    )
    def finish(a, b, o, buf, sem):
        n = 4
        q = pixels // n
        cps = [pltpu.make_async_copy(buf.at[i], o.at[pl.ds(i * q, q)], sem.at[i]) for i in range(n)]
        for i in range(n):
            buf[i] = a[pl.ds(i * q, q), :] * b[...]
            cps[i].start()
        for c in cps:
            c.wait()

    vm = pl.BlockSpec(memory_space=pltpu.VMEM)
    done = pl.pallas_call(
        finish, out_shape=jax.ShapeDtypeStruct((pixels, width), F32), in_specs=[vm, vm],
        out_specs=pl.BlockSpec(memory_space=pltpu.HBM),
        scratch_shapes=[pltpu.VMEM((4, pixels // 4, width), F32), dma((4,))],
        compiler_params=pltpu.CompilerParams(vmem_limit_bytes=28 * 2**20),
    )(current, scale)
    return done.reshape(rows, cols, width)


def solution(mesh):
    return jax.shard_map(
        functools.partial(per_device, mesh.shape["py"], mesh.shape["px"]),
        mesh=mesh,
        in_specs=(P("py", "px", None), P("py", "px"), P("py", "px", None), P("py", "px", None)),
        out_specs=P("py", "px", None),
        check_vma=False,
    )
```
